128 devices in a mesh: row: 4 (over y_hi, core), blk: 32 (over y_lo, z, x).
Axes of the slice: x: 4, y: 4 (y_hi: 2, y_lo: 2; y = y_hi * 2 + y_lo), z: 4, core: 2. Of those that a mesh axis runs over, the one named last changes fastest.
Arguments:
- coarse_cluster_means: bfloat16 [131072, 1024], P('blk', 'row'), may hold values from -16 to 16
- fine_cluster_means: bfloat16 [16384, 1024], P(('blk', 'row')), may hold values from -6 to 6
- block_panel_candidates: int32 [1024, 8], P(('blk', 'row')), may hold values from 0 to 31, all different within a row; in each aligned block of 8 rows (0 to 7, 8 to 15, ...) at most 4 rows name the same one
- softmax_heat: float32 [1], replicated, may hold values from 0.5 to 1
Outputs:
- revised_centroids: bfloat16 [16384, 1024], P(('blk', 'row'))
- log_norm: float32 [131072], P(('blk', 'row'))
The draws below stay inside these ranges and needn't reach their ends.
Inputs may be any that keep to these rules, and one draw needn't show every extreme that they name: `block_panel_candidates`: each row names 8 different panels; within the rows of one device no panel is named by more than 4 rows, and in some device one panel is named by exactly 4 rows.
All inputs are finite; a program needn't handle non-finite values.
Results may differ from the reference program's by a relative error of at most 0.013.
Values may be sent and summed in bfloat16 or wider, within the bound.
No kernel may reach another device: no remote copies, remote signals or barrier semaphores. Data moves between devices by JAX's collectives and lax.ppermute only.
A program may use at most 128 MiB of HBM per device.

```python
import math
import jax
import jax.numpy as jnp
import numpy as np
from jax import lax

FEATURE_DIMENSION = 1024
PANEL = 128
BLOCK = 128
PAIRS = 8
BLK_DEV = 8
MOST = 4
POINTS = 131072
ROW_BLOCKS = 1024
CENTROIDS = 16384
N_ROW = 4
N_BLK = 32


def draw_coarse_cluster_means(key, part):
    noise = jax.random.normal(jax.random.fold_in(key, 1), (POINTS, FEATURE_DIMENSION), jnp.float32)
    values = jnp.clip(noise, -6.0, 6.0)
    return values.astype(jnp.bfloat16)


def draw_fine_cluster_means(key, part):
    noise = jax.random.normal(jax.random.fold_in(key, 2), (CENTROIDS, FEATURE_DIMENSION), jnp.float32)
    values = jnp.clip(noise, -6.0, 6.0)
    return values.astype(jnp.bfloat16)


def shared_out(rng, own, number, rows, amount, top, most, slope):
    order = jax.random.permutation(rng, amount)
    heavy_load, common = portions_of(amount, rows * top, most, slope, True), portions_of(amount, rows * top, most, slope, False)
    places = jnp.arange(amount)

    def named(lengths, rotation):
        used = int((lengths > 0).sum())
        fixed = max(1, used // 4)
        shifted = fixed + (places - fixed + rotation * (used - fixed)) % max(1, amount - fixed)
        return jnp.zeros((amount,), jnp.int32).at[order[jnp.where(places < fixed, places, shifted)]].set(jnp.asarray(lengths, jnp.int32))

    lengths = jnp.where(number % 4 == 0, named(heavy_load, number // 4), named(common, number - number // 4 - 1))
    mixed = jax.random.permutation(jax.random.fold_in(own, 3), amount)
    donor, taker = mixed[0:amount // 2 * 2:2], mixed[1:amount // 2 * 2:2]
    margin = jnp.minimum(lengths[donor] - 1, most - lengths[taker]) // 2
    margin = jnp.where((donor == order[0]) | (taker == order[0]) | (lengths[taker] == 0), 0, jnp.maximum(margin, 0))
    shifted = jax.random.randint(jax.random.fold_in(own, 4), (amount // 2,), 0, 1 << 20) % (margin + 1)
    lengths = lengths.at[donor].add(-shifted).at[taker].add(shifted)
    labels = jnp.searchsorted(jnp.cumsum(lengths), jnp.arange(rows * top), side="right").astype(jnp.int32)
    grid = labels.reshape(top, rows).T
    grid = grid[jax.random.permutation(jax.random.fold_in(own, 1), rows)]
    rotation = jax.random.randint(jax.random.fold_in(own, 2), (rows, 1), 0, top)
    return jnp.take_along_axis(grid, (jnp.arange(top)[None, :] + rotation) % top, axis=1)


def portions_of(count, total, reach, skew, full):
    loads = [(1 << 20) // math.isqrt(standing ** skew) + 1 for standing in range(1, count + 1)]
    largest = reach if full else min(reach, max(-(-total // count), total * loads[0] // sum(loads)))
    least = 1 if total - largest >= count - 1 else 0
    counts, rest = [largest] + [least] * (count - 1), total - largest - least * (count - 1)
    while rest > 0:
        candidates = [i for i in range(1, count) if counts[i] < largest] or [i for i in range(1, count) if counts[i] < reach]
        pool, budget = sum([loads[i] for i in candidates]), rest
        for i in candidates:
            addition = min(reach - counts[i], max(1, budget * loads[i] // pool), rest)
            counts[i] = counts[i] + addition
            rest = rest - addition
    return np.array(counts)


def setup_inputs(seed: int = 0) -> dict:
    arg_keys = jax.random.split(jax.random.key(seed), 5)
    coarse_cluster_means = draw_coarse_cluster_means(jax.random.fold_in(arg_keys[4], 71), 0)
    fine_cluster_means = draw_fine_cluster_means(jax.random.fold_in(arg_keys[4], 71), 0)
    block_panel_candidates_keys = jax.random.split(jax.random.fold_in(arg_keys[2], 1), ROW_BLOCKS // BLK_DEV)
    block_panel_candidates_turns = jax.random.permutation(jax.random.fold_in(arg_keys[2], 3), ROW_BLOCKS // BLK_DEV)
    block_panel_candidates = jax.vmap(lambda own, number: shared_out(jax.random.fold_in(arg_keys[2], 2), own, number, BLK_DEV, N_BLK, PAIRS, MOST, 2))(block_panel_candidates_keys, block_panel_candidates_turns).reshape((ROW_BLOCKS, PAIRS))
    softmax_heat = jnp.clip(jnp.exp(jax.random.uniform(arg_keys[3], (1,), jnp.float32, math.log(0.5), math.log(1.0))), 0.5, 1.0)
    return dict(coarse_cluster_means=coarse_cluster_means, fine_cluster_means=fine_cluster_means, block_panel_candidates=block_panel_candidates, softmax_heat=softmax_heat)


def reference(coarse_cluster_means, fine_cluster_means, block_panel_candidates, softmax_heat):
    normalizing_multiplier = 1.0 / (softmax_heat[0] * math.sqrt(FEATURE_DIMENSION))
    panel_count = CENTROIDS // PANEL
    blocks = coarse_cluster_means.reshape(ROW_BLOCKS, BLOCK, FEATURE_DIMENSION)
    panels = fine_cluster_means.reshape(panel_count, PANEL, FEATURE_DIMENSION)
    sqnorm = lax.optimization_barrier(jnp.sum(jnp.square(fine_cluster_means.astype(jnp.float32)), axis=1)).reshape(panel_count, PANEL)

    def one_block(index):
        coarse = index // BLK_DEV % N_ROW
        chosen = (jnp.take(block_panel_candidates, index, axis=0) * N_ROW + coarse).astype(jnp.int32)
        cands = jnp.take(panels, chosen, axis=0).reshape(PAIRS * PANEL, FEATURE_DIMENSION)
        norms = jnp.take(sqnorm, chosen, axis=0).reshape(PAIRS * PANEL)
        rows = jnp.take(blocks, index, axis=0)
        dots = jnp.dot(rows.astype(jnp.float32), cands.astype(jnp.float32).T, precision=lax.Precision.HIGHEST)
        logit = (2.0 * dots - norms[None, :]) * normalizing_multiplier
        top = lax.optimization_barrier(jnp.max(logit, axis=1, keepdims=True))
        lse = top[:, 0] + jnp.log(lax.optimization_barrier(jnp.sum(jnp.exp(logit - top), axis=1)))
        assign_weight = jnp.exp(logit - lse[:, None]).astype(jnp.bfloat16)
        sums = jnp.dot(assign_weight.astype(jnp.float32).T, rows.astype(jnp.float32), precision=lax.Precision.HIGHEST)
        mass = lax.optimization_barrier(jnp.sum(assign_weight.astype(jnp.float32), axis=0))
        return (lse, chosen, sums.reshape(PAIRS, PANEL, FEATURE_DIMENSION), mass.reshape(PAIRS, PANEL))

    def step_fn(carry, index):
        acc_sums, acc_mass = carry
        lse, chosen, sums, mass = one_block(index)
        return ((acc_sums.at[chosen].add(sums), acc_mass.at[chosen].add(mass)), lse)
    init = (jnp.zeros((panel_count, PANEL, FEATURE_DIMENSION), jnp.float32), jnp.zeros((panel_count, PANEL), jnp.float32))
    (acc_sums, acc_mass), lses = lax.scan(step_fn, init, jnp.arange(ROW_BLOCKS, dtype=jnp.int32))
    sums = acc_sums.reshape(CENTROIDS, FEATURE_DIMENSION)
    mass = acc_mass.reshape(CENTROIDS)
    updated = ((sums + fine_cluster_means.astype(jnp.float32)) / (mass[:, None] + 1.0)).astype(jnp.bfloat16)
    return (updated, lses.reshape(POINTS))
```

```python
import math

import jax
import jax.numpy as jnp
from jax import lax
from jax.experimental import pallas as pl
from jax.experimental.pallas import tpu as pltpu
from jax.sharding import Mesh, PartitionSpec as P

PANEL = 128
BLOCK = 128
DIM = 1024
HALF = PANEL // 2
SLICE = 256
BLOCKS = 16
SLOTS = 8
LOW = -1e30
PACK = 4 * HALF + 16
CHUNK = HALF + 16


def moved(value, axis, by):
    size = lax.axis_size(axis)
    return lax.ppermute(value, axis, [(i, (i - by) % size) for i in range(size)])


def swapped(value):
    return lax.ppermute(value, ("c", "yl"), [(0, 0), (1, 2), (2, 1), (3, 3)])


def nt_dot(a, b):
    return lax.dot_general(a, b, (((1,), (1,)), ((), ())), preferred_element_type=jnp.float32)


def point_copies(here_ref, own, oth, x_ref, sem):
    y, c = here_ref[0], here_ref[1]
    copies = []
    for d in range(4):
        src = lax.rem(y + d, 4)
        yh, yl = src // 2, lax.rem(src, 2)
        for i, (refs, core) in enumerate(((own, c), (oth, 1 - c))):
            copies.append(
                pltpu.make_async_copy(
                    refs[d], x_ref.at[2 * yh + core, pl.ds(yl * 8, 8)], sem.at[2 * d + i]
                )
            )
    return copies


def score_kernel(
    here_ref, count_ref, list_ref, scale_ref, *refs
):
    own, oth, a_in, b_in = refs[0:4], refs[4:8], refs[8:12], refs[12:16]
    logit_ref, stat_ref = refs[16:18]
    x_ref, p_ref, l_ref, xsem, psem, lsem = refs[18:]
    xcopies = point_copies(here_ref, own, oth, x_ref, xsem)
    pcopies = []
    for dz in range(4):
        for dx in range(4):
            r = dz * 4 + dx
            pcopies.append(
                pltpu.make_async_copy(a_in[dx].at[dz], p_ref.at[r, pl.ds(0, HALF)], psem.at[2 * r])
            )
            pcopies.append(
                pltpu.make_async_copy(
                    b_in[dz].at[dx], p_ref.at[r, pl.ds(HALF, HALF)], psem.at[2 * r + 1]
                )
            )
    for copy in xcopies + pcopies:
        copy.start()
    scale = scale_ref[0]
    stat_ref[0:BLOCKS, :] = jnp.full((BLOCKS, BLOCK), LOW, jnp.float32)
    stat_ref[BLOCKS : 2 * BLOCKS, :] = jnp.zeros((BLOCKS, BLOCK), jnp.float32)
    for copy in xcopies:
        copy.wait()
    for copy in pcopies:
        copy.wait()

    def out_copy(r, t):
        return pltpu.make_async_copy(l_ref.at[r, t], logit_ref.at[r, t], lsem)

    def panel_step(r, _):
        count = count_ref[r]
        panel32 = p_ref[r].astype(jnp.float32)
        sqnorm = jnp.sum(panel32 * panel32, axis=1, keepdims=True)

        def turn(t, _):
            first, second = list_ref[r, 2 * t], list_ref[r, 2 * t + 1]
            acc = jnp.zeros((PANEL, 2 * BLOCK), jnp.float32)
            for f in range(4):
                rhs = jnp.concatenate([x_ref[f, first], x_ref[f, second]], axis=0)
                acc += nt_dot(p_ref[r, :, f * SLICE : (f + 1) * SLICE], rhs)
            logit = (2.0 * acc - sqnorm) * scale
            both = 2 * t + 1 < count
            lane = lax.broadcasted_iota(jnp.int32, (PANEL, 2 * BLOCK), 1)
            logit = jnp.where((lane < BLOCK) | both, logit, LOW)
            l_ref[r, t] = logit
            out_copy(r, t).start()

            def merge(block, part):
                old = stat_ref[pl.ds(block, 1), :]
                new = jnp.maximum(old, jnp.max(part, axis=0, keepdims=True))
                total = stat_ref[pl.ds(BLOCKS + block, 1), :] * jnp.exp(old - new)
                total += jnp.sum(jnp.exp(part - new), axis=0, keepdims=True)
                stat_ref[pl.ds(block, 1), :] = new
                stat_ref[pl.ds(BLOCKS + block, 1), :] = total

            merge(first, logit[:, :BLOCK])

            @pl.when(both)
            def _():
                merge(second, logit[:, BLOCK:])

            return 0

        return lax.fori_loop(0, (count + 1) // 2, turn, 0)

    lax.fori_loop(0, 16, panel_step, 0)

    def drain(r, _):
        def one(t, _):
            out_copy(r, t).wait()
            return 0

        return lax.fori_loop(0, (count_ref[r] + 1) // 2, one, 0)

    lax.fori_loop(0, 16, drain, 0)


def sum_kernel(here_ref, count_ref, list_ref, logit_ref, mine_ref, other_ref, *refs):
    own, oth = refs[0:4], refs[4:8]
    a_out, b_out = refs[8:12], refs[12:16]
    norm_ref = refs[16]
    x_ref, l_ref, acc_ref, mass_ref, xsem, lsem = refs[17:]
    xcopies = point_copies(here_ref, own, oth, x_ref, xsem)

    def in_copy(r, t):
        return pltpu.make_async_copy(logit_ref.at[r, t], l_ref.at[r, t], lsem.at[r])

    for copy in xcopies:
        copy.start()

    def fetch(r, _):
        def one(t, _):
            in_copy(r, t).start()
            return 0

        return lax.fori_loop(0, (count_ref[r] + 1) // 2, one, 0)

    lax.fori_loop(0, 16, fetch, 0)
    m0, s0 = mine_ref[0:BLOCKS, :], mine_ref[BLOCKS : 2 * BLOCKS, :]
    m1, s1 = other_ref[0:BLOCKS, :], other_ref[BLOCKS : 2 * BLOCKS, :]
    top = jnp.maximum(m0, m1)
    norm_ref[...] = top + jnp.log(s0 * jnp.exp(m0 - top) + s1 * jnp.exp(m1 - top))
    mass_ref[...] = jnp.zeros_like(mass_ref)
    for copy in xcopies:
        copy.wait()
    ones = jnp.ones((8, 2 * BLOCK), jnp.bfloat16)

    for dz in range(4):
        for dx in range(4):
            r = dz * 4 + dx
            turns = (count_ref[r] + 1) // 2

            def landed(t, _, r=r):
                in_copy(r, t).wait()
                return 0

            lax.fori_loop(0, turns, landed, 0)
            acc_ref[...] = jnp.zeros_like(acc_ref)

            def turn(t, mass, r=r):
                first, second = list_ref[r, 2 * t], list_ref[r, 2 * t + 1]
                norm = jnp.concatenate(
                    [norm_ref[pl.ds(first, 1), :], norm_ref[pl.ds(second, 1), :]], axis=1
                )
                weight = jnp.exp(l_ref[r, t] - norm).astype(jnp.bfloat16)
                for f in range(4):
                    rhs = jnp.concatenate([x_ref[f, first], x_ref[f, second]], axis=0)
                    acc_ref[:, f * SLICE : (f + 1) * SLICE] += jnp.dot(
                        weight, rhs, preferred_element_type=jnp.float32
                    )
                return mass + nt_dot(ones, weight)

            mass = lax.fori_loop(0, turns, turn, jnp.zeros((8, PANEL), jnp.float32))[0:1, :]
            a_out[dz][dx * HALF : (dx + 1) * HALF, :] = acc_ref[0:HALF, :].astype(jnp.bfloat16)
            b_out[dx][dz * HALF : (dz + 1) * HALF, :] = acc_ref[HALF:, :].astype(jnp.bfloat16)
            high = mass.astype(jnp.bfloat16).astype(jnp.float32)
            mass_ref[dz, dx : dx + 1, 0:PANEL] = high
            mass_ref[dz, 4 + dx : 5 + dx, 0:PANEL] = mass - high
            mass_ref[4 + dx, dz : dz + 1, 0:PANEL] = high
            mass_ref[4 + dx, 4 + dz : 5 + dz, 0:PANEL] = mass - high
    for i in range(4):
        a_out[i][4 * HALF :, :] = mass_ref[i].astype(jnp.bfloat16)
        b_out[i][4 * HALF :, :] = mass_ref[4 + i].astype(jnp.bfloat16)


def fold_kernel(*refs):
    a_in, b_in = refs[0:4], refs[4:8]
    a_out, b_out = refs[8:12], refs[12:16]
    for ins, outs in ((a_in, a_out), (b_in, b_out)):
        total = sum(ref[4 * HALF :, :].astype(jnp.float32) for ref in ins)
        mass = total[0:4, :] + total[4:8, :]
        high = mass.astype(jnp.bfloat16).astype(jnp.float32)
        for i in range(4):
            rows = slice(i * HALF, (i + 1) * HALF)
            outs[i][0:HALF, :] = sum(ref[rows, :].astype(jnp.float32) for ref in ins).astype(
                jnp.bfloat16
            )
            tail = jnp.concatenate(
                [high[i : i + 1], mass[i : i + 1] - high[i : i + 1], jnp.zeros((14, DIM), jnp.float32)],
                axis=0,
            )
            outs[i][HALF:, :] = tail.astype(jnp.bfloat16)


def finish_kernel(panel_ref, *refs):
    a_in, b_in, out_ref = refs[0:4], refs[4:8], refs[8]
    eye = lax.broadcasted_iota(jnp.int32, (HALF, PANEL), 0)
    lane = lax.broadcasted_iota(jnp.int32, (HALF, PANEL), 1)
    for h, ins in enumerate((a_in, b_in)):
        rows = slice(h * HALF, (h + 1) * HALF)
        sums = sum(ref[0:HALF, :].astype(jnp.float32) for ref in ins)
        tail = sum(ref[HALF:, 0:PANEL].astype(jnp.float32) for ref in ins)
        mass = tail[0:1, :] + tail[1:2, :]
        column = jnp.sum(jnp.where(eye + h * HALF == lane, mass, 0.0), axis=1, keepdims=True)
        panel = panel_ref[rows, :].astype(jnp.float32)
        out_ref[rows, :] = ((sums + panel) / (column + 1.0)).astype(jnp.bfloat16)


def shards(coarse_cluster_means, fine_cluster_means, block_panel_candidates, softmax_heat):
    y = 2 * lax.axis_index("yh") + lax.axis_index("yl")
    c = lax.axis_index("c")
    z, x = lax.axis_index("z"), lax.axis_index("x")
    here = jnp.stack([y, c]).astype(jnp.int32)
    scale = 1.0 / (softmax_heat * math.sqrt(DIM))

    panel = swapped(fine_cluster_means)
    half_a, half_b = panel[:HALF], panel[HALF:]
    stack_a = jnp.stack([half_a] + [moved(half_a, "z", d) for d in (1, 2, 3)])
    stack_b = jnp.stack([half_b] + [moved(half_b, "x", d) for d in (1, 2, 3)])
    all_a = [stack_a] + [moved(stack_a, "x", d) for d in (1, 2, 3)]
    all_b = [stack_b] + [moved(stack_b, "z", d) for d in (1, 2, 3)]

    groups = coarse_cluster_means.reshape(4, 8, BLOCK, SLICE)
    own = []
    for d in range(4):
        part = lax.dynamic_index_in_dim(groups, (y - d) % 4, 0, keepdims=False)
        own.append(part if d == 0 else moved(part, ("yh", "yl"), d))
    oth = [moved(part, "c", 1) for part in own]

    mine = swapped(block_panel_candidates)
    other = moved(mine, "c", 1)
    cands = jnp.where(c == 0, jnp.stack([mine, other]), jnp.stack([other, mine])).reshape(BLOCKS, 8)
    spot = ((cands // 4 % 4 - z) % 4) * 4 + (cands % 4 - x) % 4
    spot = jnp.where(cands // 16 == c, spot, -1)
    hits = jnp.any(spot[None] == jnp.arange(16, dtype=jnp.int32)[:, None, None], axis=2)
    order = jnp.cumsum(hits.astype(jnp.int32), axis=1) - 1
    count = jnp.sum(hits.astype(jnp.int32), axis=1)
    chosen = (order[:, None, :] == jnp.arange(SLOTS, dtype=jnp.int32)[None, :, None]) & hits[:, None, :]
    table = jnp.sum(jnp.where(chosen, jnp.arange(BLOCKS, dtype=jnp.int32)[None, None, :], 0), axis=2)

    smem = pl.BlockSpec(memory_space=pltpu.SMEM)
    vmem = pl.BlockSpec(memory_space=pltpu.VMEM)
    hbm = pl.BlockSpec(memory_space=pl.ANY)
    points_scratch = pltpu.VMEM((4, BLOCKS, BLOCK, SLICE), jnp.bfloat16)
    logit_scratch = pltpu.VMEM((16, SLOTS // 2, PANEL, 2 * BLOCK), jnp.float32)
    logit, stat = pl.pallas_call(
        score_kernel,
        in_specs=[smem] * 4 + [hbm] * 16,
        out_specs=[hbm, vmem],
        out_shape=[
            jax.ShapeDtypeStruct((16, SLOTS // 2, PANEL, 2 * BLOCK), jnp.float32),
            jax.ShapeDtypeStruct((2 * BLOCKS, BLOCK), jnp.float32),
        ],
        scratch_shapes=[
            points_scratch,
            pltpu.VMEM((16, PANEL, DIM), jnp.bfloat16),
            logit_scratch,
            pltpu.SemaphoreType.DMA((8,)),
            pltpu.SemaphoreType.DMA((32,)),
            pltpu.SemaphoreType.DMA,
        ],
        compiler_params=pltpu.CompilerParams(vmem_limit_bytes=40 << 20),
        name="scores",
    )(here, count, table, scale, *own, *oth, *all_a, *all_b)
    stat_other = moved(stat, "c", 1)

    packs = pl.pallas_call(
        sum_kernel,
        in_specs=[smem] * 3 + [hbm, vmem, vmem] + [hbm] * 8,
        out_specs=[vmem] * 9,
        out_shape=[jax.ShapeDtypeStruct((PACK, DIM), jnp.bfloat16)] * 8
        + [jax.ShapeDtypeStruct((BLOCKS, BLOCK), jnp.float32)],
        scratch_shapes=[
            points_scratch,
            logit_scratch,
            pltpu.VMEM((PANEL, DIM), jnp.float32),
            pltpu.VMEM((8, 16, DIM), jnp.float32),
            pltpu.SemaphoreType.DMA((8,)),
            pltpu.SemaphoreType.DMA((16,)),
        ],
        compiler_params=pltpu.CompilerParams(vmem_limit_bytes=48 << 20),
        name="sums",
    )(here, count, table, logit, stat, stat_other, *own, *oth)
    pack_a, pack_b, norm = packs[0:4], packs[4:8], packs[8]

    part_norm = lax.dynamic_slice_in_dim(norm, c * 8, 8, axis=0)
    log_norm = swapped(part_norm).reshape(8 * BLOCK)

    got_a = [pack_a[0]] + [moved(pack_a[d], "z", -d) for d in (1, 2, 3)]
    got_b = [pack_b[0]] + [moved(pack_b[d], "x", -d) for d in (1, 2, 3)]
    folded = pl.pallas_call(
        fold_kernel,
        in_specs=[vmem] * 8,
        out_specs=[vmem] * 8,
        out_shape=[jax.ShapeDtypeStruct((CHUNK, DIM), jnp.bfloat16)] * 8,
        compiler_params=pltpu.CompilerParams(vmem_limit_bytes=32 << 20),
        name="fold",
    )(*got_a, *got_b)
    part_a, part_b = folded[0:4], folded[4:8]
    last_a = [part_a[0]] + [moved(part_a[d], "x", -d) for d in (1, 2, 3)]
    last_b = [part_b[0]] + [moved(part_b[d], "z", -d) for d in (1, 2, 3)]
    revised = pl.pallas_call(
        finish_kernel,
        in_specs=[vmem] * 9,
        out_specs=vmem,
        out_shape=jax.ShapeDtypeStruct((PANEL, DIM), jnp.bfloat16),
        name="finish",
    )(panel, *last_a, *last_b)
    return (swapped(revised), log_norm)


def solution(mesh):
    split = Mesh(mesh.devices.reshape(2, 2, 2, 4, 4), ("yh", "c", "yl", "z", "x"))
    blk, row = ("yl", "z", "x"), ("yh", "c")
    return jax.shard_map(
        shards,
        mesh=split,
        in_specs=(P(blk, row), P(blk + row, None), P(blk + row, None), P()),
        out_specs=(P(blk + row, None), P(blk + row)),
        check_vma=False,
    )
```

```python
import math

import jax
import jax.numpy as jnp
from jax import lax
from jax.experimental import pallas as pl
from jax.experimental.pallas import tpu as pltpu
from jax.sharding import Mesh, PartitionSpec as P

PANEL = 128
BLOCK = 128
DIM = 1024
HALF = PANEL // 2
SLICE = 256
BLOCKS = 16
SLOTS = 8
Y = ("yh", "yl")
LOW = -1e30
HIGH = 1e30
LN2 = math.log(2.0)
PACK = 4 * HALF + 8
CHUNK = HALF + 8
STATS = 24


def moved(value, axis, by):
    size = lax.axis_size(axis)
    return lax.ppermute(value, axis, [(i, (i - by) % size) for i in range(size)])


def swapped(value):
    return lax.ppermute(value, ("c", "yl"), [(0, 0), (1, 2), (2, 1), (3, 3)])


def nt_dot(a, b):
    return lax.dot_general(a, b, (((1,), (1,)), ((), ())), preferred_element_type=jnp.float32)


def points_of(own, oth, c):
    parts = []
    for ref, core in ((own, c), (oth, 1 - c)):
        for yh in range(2):
            parts.append((ref, 16 * yh, pl.multiple_of((2 * yh + core) * SLICE, SLICE)))
    return parts


def rows_of(parts, places, features):
    return jnp.concatenate(
        [
            jnp.concatenate([ref[(place + shift) % 32] for ref, shift, _ in parts], axis=features)
            for place in places
        ],
        axis=1 - features,
    )


def by_turns(turns, run):
    for t in range(1, SLOTS // 2 + 1):
        pl.when(turns == t)(lambda t=t: run(t))


def split_kernel(*refs):
    for i in range(4):
        refs[4 + i][...] = refs[i][2 * (i % 2) : 2 * (i % 2) + 2]


def turn_kernel(ref, out):
    def one(i, _):
        out[i] = ref[i].T
        return 0

    lax.fori_loop(0, 32, one, 0, unroll=4)


def score_kernel(here_ref, count_ref, list_ref, place_ref, scale_ref, own, oth, *refs):
    a_in, b_in = refs[0:5], refs[5:10]
    l_ref, top_ref, stat_ref = refs[10:13]
    b_ref, bsem = refs[13:]

    def b_copy(dz, dx):
        src = b_in[dz].at[dx] if dz < 2 else b_in[4].at[dx] if dz == 3 else b_in[2 + dx // 2].at[dx % 2]
        return pltpu.make_async_copy(src, b_ref.at[dx, dz], bsem.at[dx, dz])

    for dx in (0, 1, 3, 2):
        for dz in range(4):
            b_copy(dz, dx).start()
    twice, once = scale_ref[0], scale_ref[1]
    parts = points_of(own, oth, here_ref[1])
    stat_ref[0:STATS, :] = jnp.full((STATS, BLOCK), LOW, jnp.float32)
    stat_ref[STATS : 2 * STATS, :] = jnp.zeros((STATS, BLOCK), jnp.float32)

    def panel_step(i, dx, a_ref, base):
        dz = base + i
        r = 4 * dx + dz
        pltpu.make_async_copy(b_in[0].at[0], b_ref.at[dx, dz], bsem.at[dx, dz]).wait()
        panel32 = jnp.concatenate([a_ref[i], b_ref[dx, dz]], axis=0).astype(jnp.float32)
        sqnorm = jnp.sum(panel32 * panel32, axis=1, keepdims=True) * once

        def run(turns):
            blocks = [list_ref[r, n] for n in range(2 * turns)]
            places = [place_ref[r, n] for n in range(2 * turns)]
            lhs = jnp.concatenate(
                [
                    jnp.concatenate(
                        [a_ref[i, :, pl.ds(at, SLICE)], b_ref[dx, dz, :, pl.ds(at, SLICE)]], axis=0
                    )
                    for _, _, at in parts
                ],
                axis=1,
            )
            old = jnp.concatenate([stat_ref[pl.ds(block, 1), :] for block in blocks], axis=1)
            total = jnp.concatenate(
                [stat_ref[pl.ds(STATS + block, 1), :] for block in blocks], axis=1
            )
            tops, adds = [], []
            for t in range(turns):
                lanes = slice(2 * t * BLOCK, 2 * (t + 1) * BLOCK)
                rhs = rows_of(parts, places[2 * t : 2 * t + 2], 0)
                logit = jnp.dot(lhs, rhs, preferred_element_type=jnp.float32) * twice - sqnorm
                top = jnp.maximum(old[:, lanes], jnp.max(logit, axis=0, keepdims=True))
                power = jnp.exp2(logit - top)
                l_ref[r, :, lanes] = power
                tops.append(top)
                adds.append(jnp.sum(power, axis=0, keepdims=True))
            new = jnp.concatenate(tops, axis=1)
            total = total * jnp.exp2(old - new) + jnp.concatenate(adds, axis=1)
            top_ref[r, :, 0 : 2 * turns * BLOCK] = jnp.broadcast_to(new, (8, 2 * turns * BLOCK))
            for j, block in enumerate(blocks):
                lanes = slice(j * BLOCK, (j + 1) * BLOCK)
                stat_ref[pl.ds(block, 1), :] = new[:, lanes]
                stat_ref[pl.ds(STATS + block, 1), :] = total[:, lanes]

        by_turns((count_ref[r] + 1) // 2, run)
        return 0

    stacks = ((0, 0, 4, 0), (1, 1, 4, 0), (3, 4, 4, 0), (2, 2, 2, 0), (2, 3, 2, 2))
    for dx, k, size, base in stacks:

        def step(i, _, dx=dx, k=k, base=base):
            return panel_step(i, dx, a_in[k], base)

        lax.fori_loop(0, size, step, 0)


def sum_kernel(
    here_ref, count_ref, list_ref, place_ref, own, oth, l_ref, top_ref, mine_ref, other_ref, *refs
):
    a_out, b_out, norm_ref = refs[0:4], refs[4:8], refs[8]
    b_ref, full_ref, mass_ref = refs[9:]
    parts = points_of(own, oth, here_ref[1])
    m0, s0 = mine_ref[0:STATS, :], mine_ref[STATS : 2 * STATS, :]
    m1, s1 = other_ref[0:STATS, :], other_ref[STATS : 2 * STATS, :]
    top = jnp.maximum(m0, m1)
    norm = top + jnp.log(s0 * jnp.exp2(m0 - top) + s1 * jnp.exp2(m1 - top)) * (1.0 / LN2)
    norm_ref[...] = norm[0:BLOCKS, :] * LN2
    row = lax.broadcasted_iota(jnp.int32, (STATS, BLOCK), 0)
    full_ref[...] = jnp.where(row < BLOCKS, norm, HIGH)
    mass_ref[...] = jnp.zeros_like(mass_ref)
    for ref in a_out:
        ref[4 * HALF :, :] = jnp.zeros((8, DIM), jnp.bfloat16)

    def panel_step(dx, _, dz):
        r = 4 * dx + dz
        arow = pl.multiple_of(dx * HALF, HALF)
        brows = slice(dz * HALF, (dz + 1) * HALF)
        turns = (count_ref[r] + 1) // 2

        @pl.when(turns == 0)
        def _():
            zeros = jnp.zeros((HALF, DIM), jnp.bfloat16)
            a_out[dz][pl.ds(arow, HALF), :] = zeros
            b_ref[dx, brows, :] = zeros

        def run(turns):
            blocks = [list_ref[r, n] for n in range(2 * turns)]
            places = [place_ref[r, n] for n in range(2 * turns)]
            norm = jnp.concatenate([full_ref[pl.ds(block, 1), :] for block in blocks], axis=1)
            lanes = slice(0, 2 * turns * BLOCK)
            factor = jnp.exp2(top_ref[r, 0:1, lanes] - norm)
            weight = (l_ref[r, :, lanes] * factor).astype(jnp.bfloat16)
            sums = jnp.dot(weight, rows_of(parts, places, 1), preferred_element_type=jnp.float32)
            sums = sums.astype(jnp.bfloat16)
            for i, (_, _, offset) in enumerate(parts):
                part = sums[:, i * SLICE : (i + 1) * SLICE]
                a_out[dz][pl.ds(arow, HALF), pl.ds(offset, SLICE)] = part[:HALF]
                b_ref[dx, brows, pl.ds(offset, SLICE)] = part[HALF:]
            mass = nt_dot(jnp.ones((8, 2 * turns * BLOCK), jnp.bfloat16), weight)[0:1, :]
            high = mass.astype(jnp.bfloat16).astype(jnp.float32)
            mass_ref[pl.ds(8 * dz + dx, 1), :] = high
            mass_ref[pl.ds(8 * dz + 4 + dx, 1), :] = mass - high

        by_turns(turns, run)
        return 0

    for i in range(4):
        lax.fori_loop(0, 4, lambda dx, _, i=i: panel_step(dx, _, i), 0)
        a_out[i][4 * HALF :, 0:PANEL] = mass_ref[8 * i : 8 * i + 8, :].astype(jnp.bfloat16)
    for i in range(4):
        b_out[i][...] = b_ref[i]


def fold_kernel(*refs):
    a_in, b_in, a_out, b_out = refs[0:4], refs[4:8], refs[8:12], refs[12:16]
    total = sum(ref[4 * HALF :, :].astype(jnp.float32) for ref in a_in)
    mass = total[0:4, :] + total[4:8, :]
    high = mass.astype(jnp.bfloat16).astype(jnp.float32)
    for i in range(4):
        rows = slice(i * HALF, (i + 1) * HALF)
        for ins, outs in ((a_in, a_out), (b_in, b_out)):
            added = sum(ref[rows, :].astype(jnp.float32) for ref in ins)
            outs[i][0:HALF, :] = added.astype(jnp.bfloat16)
        tail = jnp.concatenate(
            [high[i : i + 1], mass[i : i + 1] - high[i : i + 1], jnp.zeros((6, DIM), jnp.float32)],
            axis=0,
        )
        a_out[i][HALF:, :] = tail.astype(jnp.bfloat16)


def finish_kernel(panel_ref, *refs):
    a_in, b_in, out_ref = refs[0:4], refs[4:8], refs[8]
    row = lax.broadcasted_iota(jnp.int32, (PANEL, PANEL), 0)
    lane = lax.broadcasted_iota(jnp.int32, (PANEL, PANEL), 1)
    tail = sum(ref[HALF:, 0:PANEL].astype(jnp.float32) for ref in a_in)
    mass = tail[0:1, :] + tail[1:2, :]
    column = jnp.sum(jnp.where(row == lane, mass, 0.0), axis=1, keepdims=True)
    top = sum(ref[0:HALF, :].astype(jnp.float32) for ref in a_in)
    low = sum(ref[...].astype(jnp.float32) for ref in b_in)
    for h, sums in enumerate((top, low)):
        rows = slice(h * HALF, (h + 1) * HALF)
        panel = panel_ref[rows, :].astype(jnp.float32)
        out_ref[rows, :] = ((sums + panel) / (column[rows] + 1.0)).astype(jnp.bfloat16)


def shards(coarse_cluster_means, fine_cluster_means, block_panel_candidates, softmax_heat):
    y = 2 * lax.axis_index("yh") + lax.axis_index("yl")
    c = lax.axis_index("c")
    z, x = lax.axis_index("z"), lax.axis_index("x")
    here = jnp.stack([y, c, z, x]).astype(jnp.int32)
    once = 1.0 / (softmax_heat * (math.sqrt(DIM) * LN2))
    scale = jnp.concatenate([2.0 * once, once])

    smem = pl.BlockSpec(memory_space=pltpu.SMEM)
    vmem = pl.BlockSpec(memory_space=pltpu.VMEM)

    panel = swapped(fine_cluster_means)
    half_a, half_b = panel[:HALF], panel[HALF:]
    groups = coarse_cluster_means.reshape(4, 8, BLOCK, SLICE)
    own = [lax.dynamic_index_in_dim(groups, (y - d) % 4, 0, keepdims=False) for d in range(4)]
    own[1], own[3] = moved(own[1], Y, 1), moved(own[3], Y, 3)
    stack_a = jnp.stack([half_a] + [moved(half_a, "z", d) for d in (1, 2, 3)])
    stack_b = jnp.stack([half_b] + [moved(half_b, "x", d) for d in (1, 2, 3)])
    mine = swapped(block_panel_candidates)
    stack_a, stack_b, own, mine = lax.optimization_barrier((stack_a, stack_b, own, mine))
    other = moved(mine, "c", 1)
    next_a, last_a = moved(stack_a, "x", 1), moved(stack_a, "x", 3)
    next_b, last_b = moved(stack_b, "z", 1), moved(stack_b, "z", 3)
    own[2] = moved(own[2], Y, 2)
    own, next_a, last_a, next_b, last_b, other = lax.optimization_barrier(
        (own, next_a, last_a, next_b, last_b, other)
    )
    own = jnp.concatenate(own)
    oth = moved(own, "c", 1)
    passed = pl.pallas_call(
        split_kernel,
        in_specs=[vmem] * 4,
        out_specs=[vmem] * 4,
        out_shape=[jax.ShapeDtypeStruct((2, HALF, DIM), jnp.bfloat16)] * 4,
        name="split",
    )(next_a, last_a, next_b, last_b)
    far_a = [moved(passed[0], "x", 1), moved(passed[1], "x", 3)]
    far_b = [moved(passed[2], "z", 1), moved(passed[3], "z", 3)]
    all_a = [stack_a, next_a, *far_a, last_a]
    all_b = [stack_b, next_b, *far_b, last_b]

    cands = jnp.where(c == 0, jnp.stack([mine, other]), jnp.stack([other, mine])).reshape(BLOCKS, 8)
    spot = ((cands % 4 - x) % 4) * 4 + (cands // 4 % 4 - z) % 4
    spot = jnp.where(cands // 16 == c, spot, -1)
    hits = jnp.any(spot[None] == jnp.arange(16, dtype=jnp.int32)[:, None, None], axis=2)
    order = jnp.cumsum(hits.astype(jnp.int32), axis=1) - 1
    count = jnp.sum(hits.astype(jnp.int32), axis=1)
    chosen = (order[:, None, :] == jnp.arange(SLOTS, dtype=jnp.int32)[None, :, None]) & hits[:, None, :]
    table = BLOCKS + jnp.sum(
        jnp.where(chosen, jnp.arange(BLOCKS, dtype=jnp.int32)[None, None, :] - BLOCKS, 0), axis=2
    )
    place = (table // 8 - y) % 4 * 8 + table % 8

    turned = jax.ShapeDtypeStruct((32, SLICE, BLOCK), jnp.bfloat16)
    turn = pl.pallas_call(
        turn_kernel,
        in_specs=[vmem],
        out_specs=vmem,
        out_shape=turned,
        compiler_params=pltpu.CompilerParams(vmem_limit_bytes=16 << 20),
        name="turn",
    )
    power, top, stat = pl.pallas_call(
        score_kernel,
        in_specs=[smem] * 5 + [vmem] * 12,
        out_specs=[vmem] * 3,
        out_shape=[
            jax.ShapeDtypeStruct((16, PANEL, SLOTS * BLOCK), jnp.float32),
            jax.ShapeDtypeStruct((16, 8, SLOTS * BLOCK), jnp.float32),
            jax.ShapeDtypeStruct((2 * STATS, BLOCK), jnp.float32),
        ],
        scratch_shapes=[
            pltpu.VMEM((4, 4, HALF, DIM), jnp.bfloat16),
            pltpu.SemaphoreType.DMA((4, 4)),
        ],
        compiler_params=pltpu.CompilerParams(vmem_limit_bytes=24 << 20),
        name="scores",
    )(here, count, table, place, scale, turn(own), turn(oth), *all_a, *all_b)
    stat_other = moved(stat, "c", 1)

    packs = pl.pallas_call(
        sum_kernel,
        in_specs=[smem] * 4 + [vmem] * 6,
        out_specs=[vmem] * 9,
        out_shape=[jax.ShapeDtypeStruct((PACK, DIM), jnp.bfloat16)] * 4
        + [jax.ShapeDtypeStruct((4 * HALF, DIM), jnp.bfloat16)] * 4
        + [jax.ShapeDtypeStruct((BLOCKS, BLOCK), jnp.float32)],
        scratch_shapes=[
            pltpu.VMEM((4, 4 * HALF, DIM), jnp.bfloat16),
            pltpu.VMEM((STATS, BLOCK), jnp.float32),
            pltpu.VMEM((32, PANEL), jnp.float32),
        ],
        compiler_params=pltpu.CompilerParams(vmem_limit_bytes=24 << 20),
        name="sums",
    )(here, count, table, place, own, oth, power, top, stat, stat_other)
    pack_a, pack_b, norm = packs[0:4], packs[4:8], packs[8]

    got_a, got_b = [pack_a[0]] * 4, [pack_b[0]] * 4
    for d in (1, 3, 2):
        got_a[d] = moved(pack_a[d], "z", -d)
        got_b[d] = moved(pack_b[d], "x", -d)
    parts = pl.pallas_call(
        fold_kernel,
        in_specs=[vmem] * 8,
        out_specs=[vmem] * 8,
        out_shape=[jax.ShapeDtypeStruct((CHUNK, DIM), jnp.bfloat16)] * 4
        + [jax.ShapeDtypeStruct((HALF, DIM), jnp.bfloat16)] * 4,
        compiler_params=pltpu.CompilerParams(vmem_limit_bytes=16 << 20),
        name="fold",
    )(*got_a, *got_b)
    part_a, part_b = parts[0:4], parts[4:8]
    last_a, last_b = [part_a[0]] * 4, [part_b[0]] * 4
    for d in (1, 3, 2):
        last_a[d] = moved(part_a[d], "x", -d)
        last_b[d] = moved(part_b[d], "z", -d)
    revised = pl.pallas_call(
        finish_kernel,
        in_specs=[vmem] * 9,
        out_specs=vmem,
        out_shape=jax.ShapeDtypeStruct((PANEL, DIM), jnp.bfloat16),
        name="finish",
    )(panel, *last_a, *last_b)
    norm, revised = lax.optimization_barrier((norm, revised))
    part_norm = lax.dynamic_slice_in_dim(norm, c * 8, 8, axis=0)
    return (swapped(revised), swapped(part_norm).reshape(8 * BLOCK))


def solution(mesh):
    split = Mesh(mesh.devices.reshape(2, 2, 2, 4, 4), ("yh", "c", "yl", "z", "x"))
    blk, row = ("yl", "z", "x"), ("yh", "c")
    return jax.shard_map(
        shards,
        mesh=split,
        in_specs=(P(blk, row), P(blk + row, None), P(blk + row, None), P()),
        out_specs=(P(blk + row, None), P(blk + row)),
        check_vma=False,
    )
```

```python
import math

import jax
import jax.numpy as jnp
from jax import lax
from jax.experimental import pallas as pl
from jax.experimental.pallas import tpu as pltpu
from jax.sharding import Mesh, PartitionSpec as P

PANEL = 128
BLOCK = 128
DIM = 1024
SLICE = 256
BLOCKS = 16
PANELS = 16
SLOTS = 8
Y = ("yh", "yl")
LOW = -1e30
HIGH = 1e30
LN2 = math.log(2.0)
PACK = 4 * PANEL + 8
CHUNK = PANEL + 8
STATS = 24


def moved(value, axis, by):
    size = lax.axis_size(axis)
    return lax.ppermute(value, axis, [(i, (i - by) % size) for i in range(size)])


def swapped(value):
    return lax.ppermute(value, ("c", "yl"), [(0, 0), (1, 2), (2, 1), (3, 3)])


def nt_dot(a, b):
    return lax.dot_general(a, b, (((1,), (1,)), ((), ())), preferred_element_type=jnp.float32)


def points_of(own, oth, c):
    parts = []
    for ref, core in ((own, c), (oth, 1 - c)):
        for yh in range(2):
            parts.append((ref, 16 * yh, pl.multiple_of((2 * yh + core) * SLICE, SLICE)))
    return parts


def rows_of(parts, places, features):
    return jnp.concatenate(
        [
            jnp.concatenate([ref[(place + shift) % 32] for ref, shift, _ in parts], axis=features)
            for place in places
        ],
        axis=1 - features,
    )


def by_turns(turns, run):
    for t in range(1, SLOTS // 2 + 1):
        pl.when(turns == t)(lambda t=t: run(t))


def shifted(value, first, by):
    pairs = []
    for c in range(2):
        for z in range(4):
            for x in range(4):
                along_z = (c == 0) == first
                far = ((z + by) % 4, x) if along_z else (z, (x + by) % 4)
                pairs.append((16 * c + 4 * far[0] + far[1], 16 * c + 4 * z + x))
    return lax.ppermute(value, ("c", "z", "x"), pairs)


def turn_kernel(ref, out):
    def one(i, _):
        out[i] = ref[i].T
        return 0

    lax.fori_loop(0, 32, one, 0, unroll=4)


def score_kernel(here_ref, count_ref, list_ref, place_ref, scale_ref, own, oth, *refs):
    p_in = refs[0:4]
    l_ref, top_ref, stat_ref = refs[4:7]
    twice, once = scale_ref[0], scale_ref[1]
    parts = points_of(own, oth, here_ref[1])
    stat_ref[0:STATS, :] = jnp.full((STATS, BLOCK), LOW, jnp.float32)
    stat_ref[STATS : 2 * STATS, :] = jnp.zeros((STATS, BLOCK), jnp.float32)

    def panel_step(i, p_ref, base):
        r = base + i
        panel32 = p_ref[i].astype(jnp.float32)
        sqnorm = jnp.sum(panel32 * panel32, axis=1, keepdims=True) * once

        def run(turns):
            blocks = [list_ref[r, n] for n in range(2 * turns)]
            places = [place_ref[r, n] for n in range(2 * turns)]
            lhs = jnp.concatenate([p_ref[i, :, pl.ds(at, SLICE)] for _, _, at in parts], axis=1)
            old = jnp.concatenate([stat_ref[pl.ds(block, 1), :] for block in blocks], axis=1)
            total = jnp.concatenate(
                [stat_ref[pl.ds(STATS + block, 1), :] for block in blocks], axis=1
            )
            tops, adds = [], []
            for t in range(turns):
                lanes = slice(2 * t * BLOCK, 2 * (t + 1) * BLOCK)
                rhs = rows_of(parts, places[2 * t : 2 * t + 2], 0)
                logit = jnp.dot(lhs, rhs, preferred_element_type=jnp.float32) * twice - sqnorm
                top = jnp.maximum(old[:, lanes], jnp.max(logit, axis=0, keepdims=True))
                power = jnp.exp2(logit - top)
                l_ref[r, :, lanes] = power
                tops.append(top)
                adds.append(jnp.sum(power, axis=0, keepdims=True))
            new = jnp.concatenate(tops, axis=1)
            total = total * jnp.exp2(old - new) + jnp.concatenate(adds, axis=1)
            top_ref[r, :, 0 : 2 * turns * BLOCK] = jnp.broadcast_to(new, (8, 2 * turns * BLOCK))
            for j, block in enumerate(blocks):
                lanes = slice(j * BLOCK, (j + 1) * BLOCK)
                stat_ref[pl.ds(block, 1), :] = new[:, lanes]
                stat_ref[pl.ds(STATS + block, 1), :] = total[:, lanes]

        by_turns((count_ref[r] + 1) // 2, run)

    for k in range(4):

        def step(i, _, k=k):
            panel_step(i, p_in[k], 4 * k)
            return 0

        lax.fori_loop(0, 4, step, 0)


def sum_kernel(
    here_ref, count_ref, list_ref, place_ref, own, oth, l_ref, top_ref, mine_ref, other_ref, *refs
):
    outs, norm_ref, full_ref, mass_ref = refs[0:4], refs[4], refs[5], refs[6]
    parts = points_of(own, oth, here_ref[1])
    m0, s0 = mine_ref[0:STATS, :], mine_ref[STATS : 2 * STATS, :]
    m1, s1 = other_ref[0:STATS, :], other_ref[STATS : 2 * STATS, :]
    top = jnp.maximum(m0, m1)
    norm = top + jnp.log(s0 * jnp.exp2(m0 - top) + s1 * jnp.exp2(m1 - top)) * (1.0 / LN2)
    norm_ref[...] = norm[0:BLOCKS, :] * LN2
    row = lax.broadcasted_iota(jnp.int32, (STATS, BLOCK), 0)
    full_ref[...] = jnp.where(row < BLOCKS, norm, HIGH)
    mass_ref[...] = jnp.zeros_like(mass_ref)

    def panel_step(k, _, d):
        r = 4 * k + d
        rows = pl.multiple_of(k * PANEL, PANEL)
        turns = (count_ref[r] + 1) // 2

        @pl.when(turns == 0)
        def _():
            outs[d][pl.ds(rows, PANEL), :] = jnp.zeros((PANEL, DIM), jnp.bfloat16)

        def run(turns):
            blocks = [list_ref[r, n] for n in range(2 * turns)]
            places = [place_ref[r, n] for n in range(2 * turns)]
            norm = jnp.concatenate([full_ref[pl.ds(block, 1), :] for block in blocks], axis=1)
            lanes = slice(0, 2 * turns * BLOCK)
            factor = jnp.exp2(top_ref[r, 0:1, lanes] - norm)
            weight = (l_ref[r, :, lanes] * factor).astype(jnp.bfloat16)
            sums = jnp.dot(weight, rows_of(parts, places, 1), preferred_element_type=jnp.float32)
            sums = sums.astype(jnp.bfloat16)
            for i, (_, _, offset) in enumerate(parts):
                outs[d][pl.ds(rows, PANEL), pl.ds(offset, SLICE)] = sums[:, i * SLICE : (i + 1) * SLICE]
            mass = nt_dot(jnp.ones((8, 2 * turns * BLOCK), jnp.bfloat16), weight)[0:1, :]
            high = mass.astype(jnp.bfloat16).astype(jnp.float32)
            mass_ref[pl.ds(8 * d + k, 1), :] = high
            mass_ref[pl.ds(8 * d + 4 + k, 1), :] = mass - high

        by_turns(turns, run)
        return 0

    for d in range(4):
        lax.fori_loop(0, 4, lambda k, _, d=d: panel_step(k, _, d), 0)
        outs[d][4 * PANEL :, :] = jnp.zeros((8, DIM), jnp.bfloat16)
        outs[d][4 * PANEL :, 0:PANEL] = mass_ref[8 * d : 8 * d + 8, :].astype(jnp.bfloat16)


def fold_kernel(*refs):
    ins, outs = refs[0:4], refs[4:8]
    total = sum(ref[4 * PANEL :, 0:PANEL].astype(jnp.float32) for ref in ins)
    mass = total[0:4, :] + total[4:8, :]
    high = mass.astype(jnp.bfloat16).astype(jnp.float32)
    for i in range(4):
        rows = slice(i * PANEL, (i + 1) * PANEL)
        added = sum(ref[rows, :].astype(jnp.float32) for ref in ins)
        outs[i][0:PANEL, :] = added.astype(jnp.bfloat16)
        outs[i][PANEL:, :] = jnp.zeros((8, DIM), jnp.bfloat16)
        pieces = [high[i : i + 1], mass[i : i + 1] - high[i : i + 1]]
        pieces.append(jnp.zeros((6, PANEL), jnp.float32))
        outs[i][PANEL:, 0:PANEL] = jnp.concatenate(pieces, axis=0).astype(jnp.bfloat16)


def finish_kernel(panel_ref, *refs):
    ins, out_ref = refs[0:4], refs[4]
    row = lax.broadcasted_iota(jnp.int32, (PANEL, PANEL), 0)
    lane = lax.broadcasted_iota(jnp.int32, (PANEL, PANEL), 1)
    tail = sum(ref[PANEL:, 0:PANEL].astype(jnp.float32) for ref in ins)
    mass = tail[0:1, :] + tail[1:2, :]
    column = jnp.sum(jnp.where(row == lane, mass, 0.0), axis=1, keepdims=True)
    sums = sum(ref[0:PANEL, :].astype(jnp.float32) for ref in ins)
    panel = panel_ref[...].astype(jnp.float32)
    out_ref[...] = ((sums + panel) / (column + 1.0)).astype(jnp.bfloat16)


def shards(coarse_cluster_means, fine_cluster_means, block_panel_candidates, softmax_heat):
    yl, c = lax.axis_index("yl"), lax.axis_index("c")
    y = 2 * lax.axis_index("yh") + yl
    z, x = lax.axis_index("z"), lax.axis_index("x")
    here = jnp.stack([y, c]).astype(jnp.int32)
    once = 1.0 / (softmax_heat * (math.sqrt(DIM) * LN2))
    scale = jnp.concatenate([2.0 * once, once])
    smem = pl.BlockSpec(memory_space=pltpu.SMEM)
    vmem = pl.BlockSpec(memory_space=pltpu.VMEM)

    panel = swapped(fine_cluster_means)
    groups = coarse_cluster_means.reshape(4, 8, BLOCK, SLICE)
    own = [lax.dynamic_index_in_dim(groups, (y - d) % 4, 0, keepdims=False) for d in range(4)]
    own[1], own[3] = moved(own[1], Y, 1), moved(own[3], Y, 3)
    stack = jnp.stack([panel] + [shifted(panel, True, d) for d in (1, 2, 3)])
    mine = swapped(block_panel_candidates)
    stack, own, mine = lax.optimization_barrier((stack, own, mine))
    own[2] = moved(own[2], Y, 2)
    other = moved(mine, "c", 1)
    stacks = [stack] + [shifted(stack, False, d) for d in (1, 2, 3)]
    own = jnp.concatenate(lax.optimization_barrier((own, stacks[1], stacks[3]))[0])
    oth = moved(own, "c", 1)

    cands = jnp.where(c == 0, jnp.stack([mine, other]), jnp.stack([other, mine])).reshape(BLOCKS, 8)
    dz, dx = (cands // 4 % 4 - z) % 4, (cands % 4 - x) % 4
    spot = jnp.where(c == 0, 4 * dx + dz, 4 * dz + dx)
    spot = jnp.where(cands // 16 == c, spot, -1)
    hits = jnp.any(spot[None] == jnp.arange(PANELS, dtype=jnp.int32)[:, None, None], axis=2)
    order = jnp.cumsum(hits.astype(jnp.int32), axis=1) - 1
    count = jnp.sum(hits.astype(jnp.int32), axis=1)
    chosen = (order[:, None, :] == jnp.arange(SLOTS, dtype=jnp.int32)[None, :, None]) & hits[:, None, :]
    table = BLOCKS + jnp.sum(
        jnp.where(chosen, jnp.arange(BLOCKS, dtype=jnp.int32)[None, None, :] - BLOCKS, 0), axis=2
    )
    place = (table // 8 - y) % 4 * 8 + table % 8

    turn = pl.pallas_call(
        turn_kernel,
        in_specs=[vmem],
        out_specs=vmem,
        out_shape=jax.ShapeDtypeStruct((32, SLICE, BLOCK), jnp.bfloat16),
        compiler_params=pltpu.CompilerParams(vmem_limit_bytes=16 << 20),
        name="turn",
    )
    power, top, stat = pl.pallas_call(
        score_kernel,
        in_specs=[smem] * 5 + [vmem] * 6,
        out_specs=[vmem] * 3,
        out_shape=[
            jax.ShapeDtypeStruct((PANELS, PANEL, SLOTS * BLOCK), jnp.float32),
            jax.ShapeDtypeStruct((PANELS, 8, SLOTS * BLOCK), jnp.float32),
            jax.ShapeDtypeStruct((2 * STATS, BLOCK), jnp.float32),
        ],
        compiler_params=pltpu.CompilerParams(vmem_limit_bytes=24 << 20),
        name="scores",
    )(here, count, table, place, scale, turn(own), turn(oth), *stacks)
    stat_other = moved(stat, "c", 1)

    sums = pl.pallas_call(
        sum_kernel,
        in_specs=[smem] * 4 + [vmem] * 6,
        out_specs=[vmem] * 5,
        out_shape=[jax.ShapeDtypeStruct((PACK, DIM), jnp.bfloat16)] * 4
        + [jax.ShapeDtypeStruct((BLOCKS, BLOCK), jnp.float32)],
        scratch_shapes=[
            pltpu.VMEM((STATS, BLOCK), jnp.float32),
            pltpu.VMEM((32, PANEL), jnp.float32),
        ],
        compiler_params=pltpu.CompilerParams(vmem_limit_bytes=24 << 20),
        name="sums",
    )(here, count, table, place, own, oth, power, top, stat, stat_other)
    packs, norm = sums[0:4], sums[4]
    got = [packs[0]] + [shifted(packs[d], True, -d) for d in (1, 2, 3)]
    chunks = pl.pallas_call(
        fold_kernel,
        in_specs=[vmem] * 4,
        out_specs=[vmem] * 4,
        out_shape=[jax.ShapeDtypeStruct((CHUNK, DIM), jnp.bfloat16)] * 4,
        compiler_params=pltpu.CompilerParams(vmem_limit_bytes=16 << 20),
        name="fold",
    )(*got)
    last = [chunks[0]] + [shifted(chunks[d], False, -d) for d in (1, 2, 3)]
    revised = pl.pallas_call(
        finish_kernel,
        in_specs=[vmem] * 5,
        out_specs=vmem,
        out_shape=jax.ShapeDtypeStruct((PANEL, DIM), jnp.bfloat16),
        name="finish",
    )(panel, *last)
    norm, revised = lax.optimization_barrier((norm, revised))
    part_norm = lax.dynamic_slice_in_dim(norm, c * 8, 8, axis=0)
    return (swapped(revised), swapped(part_norm).reshape(8 * BLOCK))


def solution(mesh):
    split = Mesh(mesh.devices.reshape(2, 2, 2, 4, 4), ("yh", "c", "yl", "z", "x"))
    blk, row = ("yl", "z", "x"), ("yh", "c")
    return jax.shard_map(
        shards,
        mesh=split,
        in_specs=(P(blk, row), P(blk + row, None), P(blk + row, None), P()),
        out_specs=(P(blk + row, None), P(blk + row)),
        check_vma=False,
    )
```

```python
import functools
import math

import jax
import jax.numpy as jnp
from jax import lax
from jax.experimental import pallas as pl
from jax.experimental.pallas import tpu as pltpu
from jax.sharding import Mesh, PartitionSpec as P

PANEL = 128
BLOCK = 128
DIM = 1024
SLICE = 256
BLOCKS = 16
PANELS = 16
SLOTS = 8
Y = ("yh", "yl")
LOW = -1e30
HIGH = 1e30
LN2 = math.log(2.0)
PACK = 4 * PANEL + 8
CHUNK = PANEL + 8
STATS = 24


def moved(value, axis, by):
    size = lax.axis_size(axis)
    return lax.ppermute(value, axis, [(i, (i - by) % size) for i in range(size)])


def swapped(value):
    return lax.ppermute(value, ("c", "yl"), [(0, 0), (1, 2), (2, 1), (3, 3)])


def nt_dot(a, b):
    return lax.dot_general(a, b, (((1,), (1,)), ((), ())), preferred_element_type=jnp.float32)


def points_of(own, oth, c):
    parts = []
    for ref, core in ((own, c), (oth, 1 - c)):
        for yh in range(2):
            parts.append((ref, 16 * yh, pl.multiple_of((2 * yh + core) * SLICE, SLICE)))
    return parts


def rows_of(parts, places, features):
    return jnp.concatenate(
        [
            jnp.concatenate([ref[(place + shift) % 32] for ref, shift, _ in parts], axis=features)
            for place in places
        ],
        axis=1 - features,
    )


def by_turns(turns, run):
    for t in range(1, SLOTS // 2 + 1):
        pl.when(turns == t)(lambda t=t: run(t))


def shifted(value, first, by):
    pairs = []
    for c in range(2):
        for z in range(4):
            for x in range(4):
                along_z = (c == 0) == first
                far = ((z + by) % 4, x) if along_z else (z, (x + by) % 4)
                pairs.append((16 * c + 4 * far[0] + far[1], 16 * c + 4 * z + x))
    return lax.ppermute(value, ("c", "z", "x"), pairs)


def homeward(value, by):
    pairs = []
    for c in range(2):
        for yl in range(2):
            for z in range(4):
                for x in range(4):
                    far = (z, (x + by) % 4) if c == 0 else ((z + by) % 4, x)
                    to = 16 * (2 * yl + c) + 4 * far[0] + far[1]
                    pairs.append((16 * (2 * c + yl) + 4 * z + x, to))
    return lax.ppermute(value, ("c", "yl", "z", "x"), pairs)


def turn_kernel(ref, out):
    def one(i, _):
        out[i] = ref[i].T
        return 0

    lax.fori_loop(0, 32, one, 0, unroll=4)


def score_kernel(here_ref, count_ref, list_ref, place_ref, scale_ref, own, oth, *refs):
    p_in = refs[0:4]
    l_ref, top_ref, stat_ref = refs[4:7]
    twice, once = scale_ref[0], scale_ref[1]
    parts = points_of(own, oth, here_ref[1])
    stat_ref[0:STATS, :] = jnp.full((STATS, BLOCK), LOW, jnp.float32)
    stat_ref[STATS : 2 * STATS, :] = jnp.zeros((STATS, BLOCK), jnp.float32)

    def panel_step(i, p_ref, base):
        r = base + i
        panel32 = p_ref[i].astype(jnp.float32)
        sqnorm = jnp.sum(panel32 * panel32, axis=1, keepdims=True) * once

        def run(turns):
            blocks = [list_ref[r, n] for n in range(2 * turns)]
            places = [place_ref[r, n] for n in range(2 * turns)]
            lhs = jnp.concatenate([p_ref[i, :, pl.ds(at, SLICE)] for _, _, at in parts], axis=1)
            old = jnp.concatenate([stat_ref[pl.ds(block, 1), :] for block in blocks], axis=1)
            total = jnp.concatenate(
                [stat_ref[pl.ds(STATS + block, 1), :] for block in blocks], axis=1
            )
            tops, adds = [], []
            for t in range(turns):
                lanes = slice(2 * t * BLOCK, 2 * (t + 1) * BLOCK)
                rhs = rows_of(parts, places[2 * t : 2 * t + 2], 0)
                logit = jnp.dot(lhs, rhs, preferred_element_type=jnp.float32) * twice - sqnorm
                top = jnp.maximum(old[:, lanes], jnp.max(logit, axis=0, keepdims=True))
                power = jnp.exp2(logit - top)
                l_ref[r, :, lanes] = power
                tops.append(top)
                adds.append(jnp.sum(power, axis=0, keepdims=True))
            new = jnp.concatenate(tops, axis=1)
            total = total * jnp.exp2(old - new) + jnp.concatenate(adds, axis=1)
            top_ref[r, :, 0 : 2 * turns * BLOCK] = jnp.broadcast_to(new, (8, 2 * turns * BLOCK))
            for j, block in enumerate(blocks):
                lanes = slice(j * BLOCK, (j + 1) * BLOCK)
                stat_ref[pl.ds(block, 1), :] = new[:, lanes]
                stat_ref[pl.ds(STATS + block, 1), :] = total[:, lanes]

        by_turns((count_ref[r] + 1) // 2, run)

    for k in range(4):

        def step(i, _, k=k):
            panel_step(i, p_in[k], 4 * k)
            return 0

        lax.fori_loop(0, 4, step, 0)


def sum_kernel(
    wanted, here_ref, count_ref, list_ref, place_ref, own, oth, l_ref, top_ref, mine_ref, other_ref, *refs
):
    outs, norm_ref, full_ref, mass_ref = dict(zip(wanted, refs[0:2])), refs[2], refs[3], refs[4]
    parts = points_of(own, oth, here_ref[1])
    m0, s0 = mine_ref[0:STATS, :], mine_ref[STATS : 2 * STATS, :]
    m1, s1 = other_ref[0:STATS, :], other_ref[STATS : 2 * STATS, :]
    top = jnp.maximum(m0, m1)
    norm = top + jnp.log(s0 * jnp.exp2(m0 - top) + s1 * jnp.exp2(m1 - top)) * (1.0 / LN2)
    norm_ref[...] = norm[0:BLOCKS, :] * LN2
    row = lax.broadcasted_iota(jnp.int32, (STATS, BLOCK), 0)
    full_ref[...] = jnp.where(row < BLOCKS, norm, HIGH)
    mass_ref[...] = jnp.zeros_like(mass_ref)

    def panel_step(k, _, d):
        r = 4 * k + d
        rows = pl.multiple_of(k * PANEL, PANEL)
        turns = (count_ref[r] + 1) // 2

        @pl.when(turns == 0)
        def _():
            outs[d][pl.ds(rows, PANEL), :] = jnp.zeros((PANEL, DIM), jnp.bfloat16)

        def run(turns):
            blocks = [list_ref[r, n] for n in range(2 * turns)]
            places = [place_ref[r, n] for n in range(2 * turns)]
            norm = jnp.concatenate([full_ref[pl.ds(block, 1), :] for block in blocks], axis=1)
            lanes = slice(0, 2 * turns * BLOCK)
            factor = jnp.exp2(top_ref[r, 0:1, lanes] - norm)
            weight = (l_ref[r, :, lanes] * factor).astype(jnp.bfloat16)
            sums = jnp.dot(weight, rows_of(parts, places, 1), preferred_element_type=jnp.float32)
            sums = sums.astype(jnp.bfloat16)
            for i, (_, _, offset) in enumerate(parts):
                outs[d][pl.ds(rows, PANEL), pl.ds(offset, SLICE)] = sums[:, i * SLICE : (i + 1) * SLICE]
            mass = nt_dot(jnp.ones((8, 2 * turns * BLOCK), jnp.bfloat16), weight)[0:1, :]
            high = mass.astype(jnp.bfloat16).astype(jnp.float32)
            mass_ref[pl.ds(8 * d + k, 1), :] = high
            mass_ref[pl.ds(8 * d + 4 + k, 1), :] = mass - high

        by_turns(turns, run)
        return 0

    for d in wanted:
        lax.fori_loop(0, 4, lambda k, _, d=d: panel_step(k, _, d), 0)
        outs[d][4 * PANEL :, :] = jnp.zeros((8, DIM), jnp.bfloat16)
        outs[d][4 * PANEL :, 0:PANEL] = mass_ref[8 * d : 8 * d + 8, :].astype(jnp.bfloat16)


def fold_kernel(*refs):
    ins, outs = refs[0:4], refs[4:8]
    total = sum(ref[4 * PANEL :, 0:PANEL].astype(jnp.float32) for ref in ins)
    mass = total[0:4, :] + total[4:8, :]
    high = mass.astype(jnp.bfloat16).astype(jnp.float32)
    for i in range(4):
        rows = slice(i * PANEL, (i + 1) * PANEL)
        added = sum(ref[rows, :].astype(jnp.float32) for ref in ins)
        outs[i][0:PANEL, :] = added.astype(jnp.bfloat16)
        outs[i][PANEL:, :] = jnp.zeros((8, DIM), jnp.bfloat16)
        pieces = [high[i : i + 1], mass[i : i + 1] - high[i : i + 1]]
        pieces.append(jnp.zeros((6, PANEL), jnp.float32))
        outs[i][PANEL:, 0:PANEL] = jnp.concatenate(pieces, axis=0).astype(jnp.bfloat16)


def finish_kernel(panel_ref, *refs):
    ins, out_ref = refs[0:4], refs[4]
    row = lax.broadcasted_iota(jnp.int32, (PANEL, PANEL), 0)
    lane = lax.broadcasted_iota(jnp.int32, (PANEL, PANEL), 1)
    tail = sum(ref[PANEL:, 0:PANEL].astype(jnp.float32) for ref in ins)
    mass = tail[0:1, :] + tail[1:2, :]
    column = jnp.sum(jnp.where(row == lane, mass, 0.0), axis=1, keepdims=True)
    sums = sum(ref[0:PANEL, :].astype(jnp.float32) for ref in ins)
    panel = panel_ref[...].astype(jnp.float32)
    out_ref[...] = ((sums + panel) * (1.0 / (column + 1.0))).astype(jnp.bfloat16)


def shards(coarse_cluster_means, fine_cluster_means, block_panel_candidates, softmax_heat):
    yl, c = lax.axis_index("yl"), lax.axis_index("c")
    y = 2 * lax.axis_index("yh") + yl
    z, x = lax.axis_index("z"), lax.axis_index("x")
    here = jnp.stack([y, c]).astype(jnp.int32)
    once = 1.0 / (softmax_heat * (math.sqrt(DIM) * LN2))
    scale = jnp.concatenate([2.0 * once, once])
    smem = pl.BlockSpec(memory_space=pltpu.SMEM)
    vmem = pl.BlockSpec(memory_space=pltpu.VMEM)

    panel = swapped(fine_cluster_means)
    groups = coarse_cluster_means.reshape(4, 8, BLOCK, SLICE)
    own = [lax.dynamic_index_in_dim(groups, (y - d) % 4, 0, keepdims=False) for d in range(4)]
    own[1], own[3] = moved(own[1], Y, 1), moved(own[3], Y, 3)
    stack = jnp.stack([panel] + [shifted(panel, True, d) for d in (1, 2, 3)])
    mine = swapped(block_panel_candidates)
    stack, own, mine = lax.optimization_barrier((stack, own, mine))
    own[2] = moved(own[2], Y, 2)
    other = moved(mine, "c", 1)
    stacks = [stack] + [shifted(stack, False, d) for d in (1, 2, 3)]
    own = jnp.concatenate(lax.optimization_barrier((own, stacks[1], stacks[3]))[0])
    oth = moved(own, "c", 1)

    cands = jnp.where(c == 0, jnp.stack([mine, other]), jnp.stack([other, mine])).reshape(BLOCKS, 8)
    dz, dx = (cands // 4 % 4 - z) % 4, (cands % 4 - x) % 4
    spot = jnp.where(c == 0, 4 * dx + dz, 4 * dz + dx)
    spot = jnp.where(cands // 16 == c, spot, -1)
    hits = jnp.any(spot[None] == jnp.arange(PANELS, dtype=jnp.int32)[:, None, None], axis=2)
    order = jnp.cumsum(hits.astype(jnp.int32), axis=1) - 1
    count = jnp.sum(hits.astype(jnp.int32), axis=1)
    chosen = (order[:, None, :] == jnp.arange(SLOTS, dtype=jnp.int32)[None, :, None]) & hits[:, None, :]
    table = BLOCKS + jnp.sum(
        jnp.where(chosen, jnp.arange(BLOCKS, dtype=jnp.int32)[None, None, :] - BLOCKS, 0), axis=2
    )
    place = (table // 8 - y) % 4 * 8 + table % 8

    turn = pl.pallas_call(
        turn_kernel,
        in_specs=[vmem],
        out_specs=vmem,
        out_shape=jax.ShapeDtypeStruct((32, SLICE, BLOCK), jnp.bfloat16),
        compiler_params=pltpu.CompilerParams(vmem_limit_bytes=8 << 20),
        name="turn",
    )
    power, top, stat = pl.pallas_call(
        score_kernel,
        in_specs=[smem] * 5 + [vmem] * 6,
        out_specs=[vmem] * 3,
        out_shape=[
            jax.ShapeDtypeStruct((PANELS, PANEL, SLOTS * BLOCK), jnp.float32),
            jax.ShapeDtypeStruct((PANELS, 8, SLOTS * BLOCK), jnp.float32),
            jax.ShapeDtypeStruct((2 * STATS, BLOCK), jnp.float32),
        ],
        compiler_params=pltpu.CompilerParams(vmem_limit_bytes=8 << 20),
        name="scores",
    )(here, count, table, place, scale, turn(own), turn(oth), *stacks)
    stat_other = moved(stat, "c", 1)

    def sums_of(wanted):
        return pl.pallas_call(
            functools.partial(sum_kernel, wanted),
            in_specs=[smem] * 4 + [vmem] * 6,
            out_specs=[vmem] * 3,
            out_shape=[jax.ShapeDtypeStruct((PACK, DIM), jnp.bfloat16)] * 2
            + [jax.ShapeDtypeStruct((BLOCKS, BLOCK), jnp.float32)],
            scratch_shapes=[
                pltpu.VMEM((STATS, BLOCK), jnp.float32),
                pltpu.VMEM((32, PANEL), jnp.float32),
            ],
            compiler_params=pltpu.CompilerParams(vmem_limit_bytes=8 << 20),
            name="sums",
        )(here, count, table, place, own, oth, power, top, stat, stat_other)

    pack_far, pack_next, norm = sums_of((2, 1))
    pack_last, pack_own, _ = sums_of((3, 0))
    packs = [pack_own, pack_next, pack_far, pack_last]
    got = [packs[0]] + [shifted(packs[d], True, -d) for d in (1, 2, 3)]
    chunks = pl.pallas_call(
        fold_kernel,
        in_specs=[vmem] * 4,
        out_specs=[vmem] * 4,
        out_shape=[jax.ShapeDtypeStruct((CHUNK, DIM), jnp.bfloat16)] * 4,
        compiler_params=pltpu.CompilerParams(vmem_limit_bytes=8 << 20),
        name="fold",
    )(*got)
    norm, chunks = lax.optimization_barrier((norm, chunks))
    last = [homeward(chunks[d], d) for d in range(4)]
    part_norm = lax.dynamic_slice_in_dim(norm, c * 8, 8, axis=0)
    log_norm = swapped(part_norm).reshape(8 * BLOCK)
    revised = pl.pallas_call(
        finish_kernel,
        in_specs=[vmem] * 5,
        out_specs=vmem,
        out_shape=jax.ShapeDtypeStruct((PANEL, DIM), jnp.bfloat16),
        name="finish",
    )(fine_cluster_means, *last)
    return (revised, log_norm)


def solution(mesh):
    split = Mesh(mesh.devices.reshape(2, 2, 2, 4, 4), ("yh", "c", "yl", "z", "x"))
    blk, row = ("yl", "z", "x"), ("yh", "c")
    return jax.shard_map(
        shards,
        mesh=split,
        in_specs=(P(blk, row), P(blk + row, None), P(blk + row, None), P()),
        out_specs=(P(blk + row, None), P(blk + row)),
        check_vma=False,
    )
```

```python
import functools
import math

import jax
import jax.numpy as jnp
from jax import lax
from jax.experimental import pallas as pl
from jax.experimental.pallas import tpu as pltpu
from jax.sharding import Mesh, PartitionSpec as P

PANEL = 128
BLOCK = 128
DIM = 1024
SLICE = 256
BLOCKS = 16
PANELS = 16
SLOTS = 8
Y = ("yh", "yl")
ORDER = (0, 1, 3, 2)
LOW = -1e30
HIGH = 1e30
LN2 = math.log(2.0)
PACK = 4 * PANEL + 8
CHUNK = PANEL + 8
STATS = 24


def moved(value, axis, by):
    size = lax.axis_size(axis)
    return lax.ppermute(value, axis, [(i, (i - by) % size) for i in range(size)])


def swapped(value):
    return lax.ppermute(value, ("c", "yl"), [(0, 0), (1, 2), (2, 1), (3, 3)])


def nt_dot(a, b):
    return lax.dot_general(a, b, (((1,), (1,)), ((), ())), preferred_element_type=jnp.float32)


def points_of(own, oth, c):
    parts = []
    for ref, core in ((own, c), (oth, 1 - c)):
        for yh in range(2):
            parts.append((ref, 16 * yh, pl.multiple_of((2 * yh + core) * SLICE, SLICE)))
    return parts


def rows_of(parts, places, features):
    return jnp.concatenate(
        [
            jnp.concatenate([ref[(place + shift) % 32] for ref, shift, _ in parts], axis=features)
            for place in places
        ],
        axis=1 - features,
    )


def by_turns(turns, run):
    for t in range(1, SLOTS // 2 + 1):
        pl.when(turns == t)(lambda t=t: run(t))


def shifted(value, first, by):
    pairs = []
    for c in range(2):
        for z in range(4):
            for x in range(4):
                along_z = (c == 0) == first
                far = ((z + by) % 4, x) if along_z else (z, (x + by) % 4)
                pairs.append((16 * c + 4 * far[0] + far[1], 16 * c + 4 * z + x))
    return lax.ppermute(value, ("c", "z", "x"), pairs)


def homeward(value, by):
    pairs = []
    for c in range(2):
        for yl in range(2):
            for z in range(4):
                for x in range(4):
                    far = (z, (x + by) % 4) if c == 0 else ((z + by) % 4, x)
                    to = 16 * (2 * yl + c) + 4 * far[0] + far[1]
                    pairs.append((16 * (2 * c + yl) + 4 * z + x, to))
    return lax.ppermute(value, ("c", "yl", "z", "x"), pairs)


def turn_kernel(ref, out):
    def one(i, _):
        out[i] = ref[i].T
        return 0

    lax.fori_loop(0, 32, one, 0, unroll=4)


def score_kernel(
    base, here_ref, count_ref, list_ref, place_ref, scale_ref, own, oth, before_ref, *refs
):
    p_in, (l_ref, top_ref, stat_ref) = refs[:-3], refs[-3:]
    twice, once = scale_ref[0], scale_ref[1]
    parts = points_of(own, oth, here_ref[1])
    stat_ref[...] = before_ref[...]

    def panel_step(i, p_ref, start):
        r = start + i
        row = r - 4 * base
        panel32 = p_ref[i].astype(jnp.float32)
        sqnorm = jnp.sum(panel32 * panel32, axis=1, keepdims=True) * once

        def run(turns):
            blocks = [list_ref[r, n] for n in range(2 * turns)]
            places = [place_ref[r, n] for n in range(2 * turns)]
            lhs = jnp.concatenate([p_ref[i, :, pl.ds(at, SLICE)] for _, _, at in parts], axis=1)
            old = jnp.concatenate([stat_ref[pl.ds(block, 1), :] for block in blocks], axis=1)
            total = jnp.concatenate(
                [stat_ref[pl.ds(STATS + block, 1), :] for block in blocks], axis=1
            )
            tops, adds = [], []
            for t in range(turns):
                lanes = slice(2 * t * BLOCK, 2 * (t + 1) * BLOCK)
                rhs = rows_of(parts, places[2 * t : 2 * t + 2], 0)
                logit = jnp.dot(lhs, rhs, preferred_element_type=jnp.float32) * twice - sqnorm
                top = jnp.maximum(old[:, lanes], jnp.max(logit, axis=0, keepdims=True))
                power = jnp.exp2(logit - top)
                l_ref[row, :, lanes] = power
                tops.append(top)
                adds.append(jnp.sum(power, axis=0, keepdims=True))
            new = jnp.concatenate(tops, axis=1)
            total = total * jnp.exp2(old - new) + jnp.concatenate(adds, axis=1)
            top_ref[row, :, 0 : 2 * turns * BLOCK] = jnp.broadcast_to(new, (8, 2 * turns * BLOCK))
            for j, block in enumerate(blocks):
                lanes = slice(j * BLOCK, (j + 1) * BLOCK)
                stat_ref[pl.ds(block, 1), :] = new[:, lanes]
                stat_ref[pl.ds(STATS + block, 1), :] = total[:, lanes]

        by_turns((count_ref[r] + 1) // 2, run)

    for k, p_ref in enumerate(p_in):

        def step(i, _, k=k, p_ref=p_ref):
            panel_step(i, p_ref, 4 * (base + k))
            return 0

        lax.fori_loop(0, 4, step, 0)


def sum_kernel(
    wanted, here_ref, count_ref, list_ref, place_ref, own, oth, mine_ref, other_ref, *refs
):
    scored, refs = ((refs[0], refs[1], 0), (refs[2], refs[3], 3)), refs[4:]
    outs, norm_ref, full_ref, mass_ref = dict(zip(wanted, refs[0:2])), refs[2], refs[3], refs[4]
    parts = points_of(own, oth, here_ref[1])
    m0, s0 = mine_ref[0:STATS, :], mine_ref[STATS : 2 * STATS, :]
    m1, s1 = other_ref[0:STATS, :], other_ref[STATS : 2 * STATS, :]
    top = jnp.maximum(m0, m1)
    norm = top + jnp.log(s0 * jnp.exp2(m0 - top) + s1 * jnp.exp2(m1 - top)) * (1.0 / LN2)
    norm_ref[...] = norm[0:BLOCKS, :] * LN2
    row = lax.broadcasted_iota(jnp.int32, (STATS, BLOCK), 0)
    full_ref[...] = jnp.where(row < BLOCKS, norm, HIGH)
    mass_ref[...] = jnp.zeros_like(mass_ref)

    def panel_step(k, d, l_ref, top_ref, base):
        r = 4 * k + d
        row = r - 4 * base
        rows = pl.multiple_of(k * PANEL, PANEL)
        turns = (count_ref[r] + 1) // 2

        @pl.when(turns == 0)
        def _():
            outs[d][pl.ds(rows, PANEL), :] = jnp.zeros((PANEL, DIM), jnp.bfloat16)

        def run(turns):
            blocks = [list_ref[r, n] for n in range(2 * turns)]
            places = [place_ref[r, n] for n in range(2 * turns)]
            norm = jnp.concatenate([full_ref[pl.ds(block, 1), :] for block in blocks], axis=1)
            lanes = slice(0, 2 * turns * BLOCK)
            factor = jnp.exp2(top_ref[row, 0:1, lanes] - norm)
            weight = (l_ref[row, :, lanes] * factor).astype(jnp.bfloat16)
            sums = jnp.dot(weight, rows_of(parts, places, 1), preferred_element_type=jnp.float32)
            sums = sums.astype(jnp.bfloat16)
            for i, (_, _, offset) in enumerate(parts):
                outs[d][pl.ds(rows, PANEL), pl.ds(offset, SLICE)] = sums[:, i * SLICE : (i + 1) * SLICE]
            mass = nt_dot(jnp.ones((8, 2 * turns * BLOCK), jnp.bfloat16), weight)[0:1, :]
            high = mass.astype(jnp.bfloat16).astype(jnp.float32)
            mass_ref[pl.ds(8 * d + k, 1), :] = high
            mass_ref[pl.ds(8 * d + 4 + k, 1), :] = mass - high

        by_turns(turns, run)
        return 0

    for d in wanted:
        for l_ref, top_ref, base in scored:

            def step(k, _, d=d, l_ref=l_ref, top_ref=top_ref, base=base):
                return panel_step(k, d, l_ref, top_ref, base)

            lax.fori_loop(base, 3 if base == 0 else 4, step, 0)
        outs[d][4 * PANEL :, :] = jnp.zeros((8, DIM), jnp.bfloat16)
        outs[d][4 * PANEL :, 0:PANEL] = mass_ref[8 * d : 8 * d + 8, :].astype(jnp.bfloat16)


def fold_kernel(*refs):
    ins, outs = refs[0:4], refs[4:8]
    total = sum(ref[4 * PANEL :, 0:PANEL].astype(jnp.float32) for ref in ins)
    mass = total[0:4, :] + total[4:8, :]
    high = mass.astype(jnp.bfloat16).astype(jnp.float32)
    for i in range(4):
        rows = slice(i * PANEL, (i + 1) * PANEL)
        added = sum(ref[rows, :].astype(jnp.float32) for ref in ins)
        outs[i][0:PANEL, :] = added.astype(jnp.bfloat16)
        outs[i][PANEL:, :] = jnp.zeros((8, DIM), jnp.bfloat16)
        pieces = [high[i : i + 1], mass[i : i + 1] - high[i : i + 1]]
        pieces.append(jnp.zeros((6, PANEL), jnp.float32))
        outs[i][PANEL:, 0:PANEL] = jnp.concatenate(pieces, axis=0).astype(jnp.bfloat16)


def finish_kernel(panel_ref, *refs):
    ins, out_ref = refs[0:4], refs[4]
    row = lax.broadcasted_iota(jnp.int32, (PANEL, PANEL), 0)
    lane = lax.broadcasted_iota(jnp.int32, (PANEL, PANEL), 1)
    tail = sum(ref[PANEL:, 0:PANEL].astype(jnp.float32) for ref in ins)
    mass = tail[0:1, :] + tail[1:2, :]
    column = jnp.sum(jnp.where(row == lane, mass, 0.0), axis=1, keepdims=True)
    sums = sum(ref[0:PANEL, :].astype(jnp.float32) for ref in ins)
    panel = panel_ref[...].astype(jnp.float32)
    out_ref[...] = ((sums + panel) * (1.0 / (column + 1.0))).astype(jnp.bfloat16)


def shards(coarse_cluster_means, fine_cluster_means, block_panel_candidates, softmax_heat):
    yl, c = lax.axis_index("yl"), lax.axis_index("c")
    y = 2 * lax.axis_index("yh") + yl
    z, x = lax.axis_index("z"), lax.axis_index("x")
    here = jnp.stack([y, c]).astype(jnp.int32)
    once = 1.0 / (softmax_heat * (math.sqrt(DIM) * LN2))
    scale = jnp.concatenate([2.0 * once, once])
    smem = pl.BlockSpec(memory_space=pltpu.SMEM)
    vmem = pl.BlockSpec(memory_space=pltpu.VMEM)

    panel = swapped(fine_cluster_means)
    groups = coarse_cluster_means.reshape(4, 8, BLOCK, SLICE)
    own = [lax.dynamic_index_in_dim(groups, (y - d) % 4, 0, keepdims=False) for d in range(4)]
    own[1], own[3] = moved(own[1], Y, 1), moved(own[3], Y, 3)
    stack = jnp.stack([panel] + [shifted(panel, True, d) for d in (1, 2, 3)])
    mine = swapped(block_panel_candidates)
    stack, own, mine = lax.optimization_barrier((stack, own, mine))
    own[2] = moved(own[2], Y, 2)
    other = moved(mine, "c", 1)
    stacks = [stack] + [shifted(stack, False, d) for d in ORDER[1:]]
    own = jnp.concatenate(lax.optimization_barrier((own, stacks[1], stacks[2]))[0])
    oth = moved(own, "c", 1)

    cands = jnp.where(c == 0, jnp.stack([mine, other]), jnp.stack([other, mine])).reshape(BLOCKS, 8)
    dz, dx = (cands // 4 % 4 - z) % 4, (cands % 4 - x) % 4
    d1, d2 = jnp.where(c == 0, dz, dx), jnp.where(c == 0, dx, dz)
    spot = 4 * jnp.where(d2 >= 2, 5 - d2, d2) + d1
    spot = jnp.where(cands // 16 == c, spot, -1)
    hits = jnp.any(spot[None] == jnp.arange(PANELS, dtype=jnp.int32)[:, None, None], axis=2)
    order = jnp.cumsum(hits.astype(jnp.int32), axis=1) - 1
    count = jnp.sum(hits.astype(jnp.int32), axis=1)
    chosen = (order[:, None, :] == jnp.arange(SLOTS, dtype=jnp.int32)[None, :, None]) & hits[:, None, :]
    table = BLOCKS + jnp.sum(
        jnp.where(chosen, jnp.arange(BLOCKS, dtype=jnp.int32)[None, None, :] - BLOCKS, 0), axis=2
    )
    place = (table // 8 - y) % 4 * 8 + table % 8

    turn = pl.pallas_call(
        turn_kernel,
        in_specs=[vmem],
        out_specs=vmem,
        out_shape=jax.ShapeDtypeStruct((32, SLICE, BLOCK), jnp.bfloat16),
        compiler_params=pltpu.CompilerParams(vmem_limit_bytes=8 << 20),
        name="turn",
    )
    def scores_of(base, stat, held):
        return pl.pallas_call(
            functools.partial(score_kernel, base),
            in_specs=[smem] * 5 + [vmem] * (3 + len(held)),
            out_specs=[vmem] * 3,
            out_shape=[
                jax.ShapeDtypeStruct((4 * len(held), PANEL, SLOTS * BLOCK), jnp.float32),
                jax.ShapeDtypeStruct((4 * len(held), 8, SLOTS * BLOCK), jnp.float32),
                jax.ShapeDtypeStruct((2 * STATS, BLOCK), jnp.float32),
            ],
            compiler_params=pltpu.CompilerParams(vmem_limit_bytes=8 << 20),
            name="scores",
        )(here, count, table, place, scale, own_t, oth_t, stat, *held)

    own_t, oth_t = turn(own), turn(oth)
    low = jnp.full((STATS, BLOCK), LOW, jnp.float32)
    *near, stat = scores_of(0, jnp.concatenate([low, jnp.zeros_like(low)]), stacks[0:3])
    *far, stat = scores_of(3, stat, stacks[3:4])
    stat_other = moved(stat, "c", 1)

    def sums_of(wanted, stat):
        return pl.pallas_call(
            functools.partial(sum_kernel, wanted),
            in_specs=[smem] * 4 + [vmem] * 8,
            out_specs=[vmem] * 3,
            out_shape=[jax.ShapeDtypeStruct((PACK, DIM), jnp.bfloat16)] * 2
            + [jax.ShapeDtypeStruct((BLOCKS, BLOCK), jnp.float32)],
            scratch_shapes=[
                pltpu.VMEM((STATS, BLOCK), jnp.float32),
                pltpu.VMEM((32, PANEL), jnp.float32),
            ],
            compiler_params=pltpu.CompilerParams(vmem_limit_bytes=8 << 20),
            cost_estimate=pl.CostEstimate(
                flops=4_000_000_000, transcendentals=0, bytes_accessed=16_000_000
            ),
            name="sums",
        )(here, count, table, place, own, oth, stat, stat_other, *near, *far)

    pack_last, pack_own, norm = sums_of((3, 0), stat)
    pack_far, pack_next, _ = sums_of((2, 1), stat)
    packs = [pack_own, pack_next, pack_far, pack_last]
    got = [packs[0]] + [shifted(packs[d], True, -d) for d in (1, 2, 3)]
    chunks = pl.pallas_call(
        fold_kernel,
        in_specs=[vmem] * 4,
        out_specs=[vmem] * 4,
        out_shape=[jax.ShapeDtypeStruct((CHUNK, DIM), jnp.bfloat16)] * 4,
        compiler_params=pltpu.CompilerParams(vmem_limit_bytes=8 << 20),
        name="fold",
    )(*got)
    norm, chunks = lax.optimization_barrier((norm, chunks))
    last = [homeward(chunk, d) for chunk, d in zip(chunks, ORDER)]
    part_norm = lax.dynamic_slice_in_dim(norm, c * 8, 8, axis=0)
    log_norm = swapped(part_norm).reshape(8 * BLOCK)
    revised = pl.pallas_call(
        finish_kernel,
        in_specs=[vmem] * 5,
        out_specs=vmem,
        out_shape=jax.ShapeDtypeStruct((PANEL, DIM), jnp.bfloat16),
        compiler_params=pltpu.CompilerParams(vmem_limit_bytes=4 << 20),
        name="finish",
    )(fine_cluster_means, *last)
    return (revised, log_norm)


def solution(mesh):
    split = Mesh(mesh.devices.reshape(2, 2, 2, 4, 4), ("yh", "c", "yl", "z", "x"))
    blk, row = ("yl", "z", "x"), ("yh", "c")
    return jax.shard_map(
        shards,
        mesh=split,
        in_specs=(P(blk, row), P(blk + row, None), P(blk + row, None), P()),
        out_specs=(P(blk + row, None), P(blk + row)),
        check_vma=False,
    )
```

```python
import functools
import math

import jax
import jax.numpy as jnp
from jax import lax
from jax.experimental import pallas as pl
from jax.experimental.pallas import tpu as pltpu
from jax.sharding import Mesh, PartitionSpec as P

PANEL = 128
BLOCK = 128
DIM = 1024
SLICE = 256
BLOCKS = 16
PANELS = 16
SLOTS = 8
Y = ("yh", "yl")
ORDER = (0, 1, 3, 2)
LOW = -1e30
HIGH = 1e30
LN2 = math.log(2.0)
PACK = 4 * PANEL + 8
CHUNK = PANEL + 8
STATS = 24


def moved(value, axis, by):
    size = lax.axis_size(axis)
    return lax.ppermute(value, axis, [(i, (i - by) % size) for i in range(size)])


def swapped(value):
    return lax.ppermute(value, ("c", "yl"), [(0, 0), (1, 2), (2, 1), (3, 3)])


def nt_dot(a, b):
    return lax.dot_general(a, b, (((1,), (1,)), ((), ())), preferred_element_type=jnp.float32)


def points_of(own, oth, c):
    parts = []
    for ref, core in ((own, c), (oth, 1 - c)):
        for yh in range(2):
            parts.append((ref, 16 * yh, pl.multiple_of((2 * yh + core) * SLICE, SLICE)))
    return parts


def rows_of(parts, places, features):
    return jnp.concatenate(
        [
            jnp.concatenate([ref[(place + shift) % 32] for ref, shift, _ in parts], axis=features)
            for place in places
        ],
        axis=1 - features,
    )


def by_turns(turns, run):
    for t in range(1, SLOTS // 2 + 1):
        pl.when(turns == t)(lambda t=t: run(t))


def shifted(value, first, by):
    pairs = []
    for c in range(2):
        for z in range(4):
            for x in range(4):
                along_z = (c == 0) == first
                far = ((z + by) % 4, x) if along_z else (z, (x + by) % 4)
                pairs.append((16 * c + 4 * far[0] + far[1], 16 * c + 4 * z + x))
    return lax.ppermute(value, ("c", "z", "x"), pairs)


def homeward(value, by):
    pairs = []
    for c in range(2):
        for yl in range(2):
            for z in range(4):
                for x in range(4):
                    far = (z, (x + by) % 4) if c == 0 else ((z + by) % 4, x)
                    to = 16 * (2 * yl + c) + 4 * far[0] + far[1]
                    pairs.append((16 * (2 * c + yl) + 4 * z + x, to))
    return lax.ppermute(value, ("c", "yl", "z", "x"), pairs)


def join_kernel(*refs):
    for d in range(4):
        refs[6][8 * d : 8 * d + 8] = refs[d][...]


def turn_kernel(ref, out):
    def one(i, _):
        out[i] = ref[i].T
        return 0

    lax.fori_loop(0, 32, one, 0, unroll=4)


def score_kernel(
    base, here_ref, count_ref, list_ref, place_ref, scale_ref, own, oth, before_ref, *refs
):
    p_in, (l_ref, top_ref, stat_ref) = refs[:-3], refs[-3:]
    twice, once = scale_ref[0], scale_ref[1]
    parts = points_of(own, oth, here_ref[1])
    stat_ref[...] = before_ref[...]

    def panel_step(i, p_ref, start):
        r = start + i
        row = r - 4 * base
        panel32 = p_ref[i].astype(jnp.float32)
        sqnorm = jnp.sum(panel32 * panel32, axis=1, keepdims=True) * once

        def run(turns):
            blocks = [list_ref[r, n] for n in range(2 * turns)]
            places = [place_ref[r, n] for n in range(2 * turns)]
            lhs = jnp.concatenate([p_ref[i, :, pl.ds(at, SLICE)] for _, _, at in parts], axis=1)
            old = jnp.concatenate([stat_ref[pl.ds(block, 1), :] for block in blocks], axis=1)
            total = jnp.concatenate(
                [stat_ref[pl.ds(STATS + block, 1), :] for block in blocks], axis=1
            )
            tops, adds = [], []
            for t in range(turns):
                lanes = slice(2 * t * BLOCK, 2 * (t + 1) * BLOCK)
                rhs = rows_of(parts, places[2 * t : 2 * t + 2], 0)
                logit = jnp.dot(lhs, rhs, preferred_element_type=jnp.float32) * twice - sqnorm
                top = jnp.maximum(old[:, lanes], jnp.max(logit, axis=0, keepdims=True))
                power = jnp.exp2(logit - top)
                l_ref[row, :, lanes] = power
                tops.append(top)
                adds.append(jnp.sum(power, axis=0, keepdims=True))
            new = jnp.concatenate(tops, axis=1)
            total = total * jnp.exp2(old - new) + jnp.concatenate(adds, axis=1)
            top_ref[row, :, 0 : 2 * turns * BLOCK] = jnp.broadcast_to(new, (8, 2 * turns * BLOCK))
            for j, block in enumerate(blocks):
                lanes = slice(j * BLOCK, (j + 1) * BLOCK)
                stat_ref[pl.ds(block, 1), :] = new[:, lanes]
                stat_ref[pl.ds(STATS + block, 1), :] = total[:, lanes]

        by_turns((count_ref[r] + 1) // 2, run)

    for k, p_ref in enumerate(p_in):

        def step(i, _, k=k, p_ref=p_ref):
            panel_step(i, p_ref, 4 * (base + k))
            return 0

        lax.fori_loop(0, 4, step, 0)


def sum_kernel(
    wanted, here_ref, count_ref, list_ref, place_ref, own, oth, mine_ref, other_ref, *refs
):
    scored, refs = ((refs[0], refs[1], 0), (refs[2], refs[3], 3)), refs[4:]
    outs, (norm_ref, full_ref, mass_ref) = dict(zip(wanted, refs)), refs[len(wanted) :]
    parts = points_of(own, oth, here_ref[1])
    m0, s0 = mine_ref[0:STATS, :], mine_ref[STATS : 2 * STATS, :]
    m1, s1 = other_ref[0:STATS, :], other_ref[STATS : 2 * STATS, :]
    top = jnp.maximum(m0, m1)
    norm = top + jnp.log(s0 * jnp.exp2(m0 - top) + s1 * jnp.exp2(m1 - top)) * (1.0 / LN2)
    norm_ref[...] = norm[0:BLOCKS, :] * LN2
    row = lax.broadcasted_iota(jnp.int32, (STATS, BLOCK), 0)
    full_ref[...] = jnp.where(row < BLOCKS, norm, HIGH)
    mass_ref[...] = jnp.zeros_like(mass_ref)

    def panel_step(k, d, l_ref, top_ref, base):
        r = 4 * k + d
        row = r - 4 * base
        rows = pl.multiple_of(k * PANEL, PANEL)
        turns = (count_ref[r] + 1) // 2

        @pl.when(turns == 0)
        def _():
            outs[d][pl.ds(rows, PANEL), :] = jnp.zeros((PANEL, DIM), jnp.bfloat16)

        def run(turns):
            blocks = [list_ref[r, n] for n in range(2 * turns)]
            places = [place_ref[r, n] for n in range(2 * turns)]
            norm = jnp.concatenate([full_ref[pl.ds(block, 1), :] for block in blocks], axis=1)
            lanes = slice(0, 2 * turns * BLOCK)
            factor = jnp.exp2(top_ref[row, 0:1, lanes] - norm)
            weight = (l_ref[row, :, lanes] * factor).astype(jnp.bfloat16)
            sums = jnp.dot(weight, rows_of(parts, places, 1), preferred_element_type=jnp.float32)
            sums = sums.astype(jnp.bfloat16)
            for i, (_, _, offset) in enumerate(parts):
                outs[d][pl.ds(rows, PANEL), pl.ds(offset, SLICE)] = sums[:, i * SLICE : (i + 1) * SLICE]
            mass = nt_dot(jnp.ones((8, 2 * turns * BLOCK), jnp.bfloat16), weight)[0:1, :]
            high = mass.astype(jnp.bfloat16).astype(jnp.float32)
            mass_ref[pl.ds(8 * d + k, 1), :] = high
            mass_ref[pl.ds(8 * d + 4 + k, 1), :] = mass - high

        by_turns(turns, run)
        return 0

    for d in wanted:
        for l_ref, top_ref, base in scored:

            def step(k, _, d=d, l_ref=l_ref, top_ref=top_ref, base=base):
                return panel_step(k, d, l_ref, top_ref, base)

            lax.fori_loop(base, 3 if base == 0 else 4, step, 0)
        outs[d][4 * PANEL :, :] = jnp.zeros((8, DIM), jnp.bfloat16)
        outs[d][4 * PANEL :, 0:PANEL] = mass_ref[8 * d : 8 * d + 8, :].astype(jnp.bfloat16)


def fold_kernel(*refs):
    ins, outs = refs[0:4], refs[4:8]
    total = sum(ref[4 * PANEL :, 0:PANEL].astype(jnp.float32) for ref in ins)
    mass = total[0:4, :] + total[4:8, :]
    high = mass.astype(jnp.bfloat16).astype(jnp.float32)
    for i in range(4):
        rows = slice(i * PANEL, (i + 1) * PANEL)
        added = sum(ref[rows, :].astype(jnp.float32) for ref in ins)
        outs[i][0:PANEL, :] = added.astype(jnp.bfloat16)
        outs[i][PANEL:, :] = jnp.zeros((8, DIM), jnp.bfloat16)
        pieces = [high[i : i + 1], mass[i : i + 1] - high[i : i + 1]]
        pieces.append(jnp.zeros((6, PANEL), jnp.float32))
        outs[i][PANEL:, 0:PANEL] = jnp.concatenate(pieces, axis=0).astype(jnp.bfloat16)


def finish_kernel(panel_ref, *refs):
    ins, out_ref = refs[0:4], refs[4]
    row = lax.broadcasted_iota(jnp.int32, (PANEL, PANEL), 0)
    lane = lax.broadcasted_iota(jnp.int32, (PANEL, PANEL), 1)
    tail = sum(ref[PANEL:, 0:PANEL].astype(jnp.float32) for ref in ins)
    mass = tail[0:1, :] + tail[1:2, :]
    column = jnp.sum(jnp.where(row == lane, mass, 0.0), axis=1, keepdims=True)
    sums = sum(ref[0:PANEL, :].astype(jnp.float32) for ref in ins)
    panel = panel_ref[...].astype(jnp.float32)
    out_ref[...] = ((sums + panel) * (1.0 / (column + 1.0))).astype(jnp.bfloat16)


def shards(coarse_cluster_means, fine_cluster_means, block_panel_candidates, softmax_heat):
    yl, c = lax.axis_index("yl"), lax.axis_index("c")
    y = 2 * lax.axis_index("yh") + yl
    z, x = lax.axis_index("z"), lax.axis_index("x")
    here = jnp.stack([y, c]).astype(jnp.int32)
    once = 1.0 / (softmax_heat * (math.sqrt(DIM) * LN2))
    scale = jnp.concatenate([2.0 * once, once])
    smem = pl.BlockSpec(memory_space=pltpu.SMEM)
    vmem = pl.BlockSpec(memory_space=pltpu.VMEM)

    panel = swapped(fine_cluster_means)
    groups = coarse_cluster_means.reshape(4, 8, BLOCK, SLICE)
    own = [lax.dynamic_index_in_dim(groups, (y - d) % 4, 0, keepdims=False) for d in range(4)]
    own[1], own[3] = moved(own[1], Y, 1), moved(own[3], Y, 3)
    stack = jnp.stack([panel] + [shifted(panel, True, d) for d in (1, 2, 3)])
    mine = swapped(block_panel_candidates)
    stack, own, mine = lax.optimization_barrier((stack, own, mine))
    own[2] = moved(own[2], Y, 2)
    other = moved(mine, "c", 1)
    stacks = [stack] + [shifted(stack, False, d) for d in ORDER[1:]]
    own = pl.pallas_call(
        join_kernel,
        in_specs=[vmem] * 4 + [pl.BlockSpec(memory_space=pl.ANY)] * 2,
        out_specs=vmem,
        out_shape=jax.ShapeDtypeStruct((32, BLOCK, SLICE), jnp.bfloat16),
        compiler_params=pltpu.CompilerParams(vmem_limit_bytes=8 << 20),
        name="join",
    )(*own, stacks[1], stacks[2])
    oth = moved(own, "c", 1)

    cands = jnp.where(c == 0, jnp.stack([mine, other]), jnp.stack([other, mine])).reshape(BLOCKS, 8)
    dz, dx = (cands // 4 % 4 - z) % 4, (cands % 4 - x) % 4
    d1, d2 = jnp.where(c == 0, dz, dx), jnp.where(c == 0, dx, dz)
    spot = 4 * jnp.where(d2 >= 2, 5 - d2, d2) + d1
    spot = jnp.where(cands // 16 == c, spot, -1)
    hits = jnp.any(spot[None] == jnp.arange(PANELS, dtype=jnp.int32)[:, None, None], axis=2)
    order = jnp.cumsum(hits.astype(jnp.int32), axis=1) - 1
    count = jnp.sum(hits.astype(jnp.int32), axis=1)
    chosen = (order[:, None, :] == jnp.arange(SLOTS, dtype=jnp.int32)[None, :, None]) & hits[:, None, :]
    table = BLOCKS + jnp.sum(
        jnp.where(chosen, jnp.arange(BLOCKS, dtype=jnp.int32)[None, None, :] - BLOCKS, 0), axis=2
    )
    place = (table // 8 - y) % 4 * 8 + table % 8

    turn = pl.pallas_call(
        turn_kernel,
        in_specs=[vmem],
        out_specs=vmem,
        out_shape=jax.ShapeDtypeStruct((32, SLICE, BLOCK), jnp.bfloat16),
        compiler_params=pltpu.CompilerParams(vmem_limit_bytes=8 << 20),
        name="turn",
    )
    def scores_of(base, stat, held):
        return pl.pallas_call(
            functools.partial(score_kernel, base),
            in_specs=[smem] * 5 + [vmem] * (3 + len(held)),
            out_specs=[vmem] * 3,
            out_shape=[
                jax.ShapeDtypeStruct((4 * len(held), PANEL, SLOTS * BLOCK), jnp.float32),
                jax.ShapeDtypeStruct((4 * len(held), 8, SLOTS * BLOCK), jnp.float32),
                jax.ShapeDtypeStruct((2 * STATS, BLOCK), jnp.float32),
            ],
            compiler_params=pltpu.CompilerParams(vmem_limit_bytes=8 << 20),
            name="scores",
        )(here, count, table, place, scale, own_t, oth_t, stat, *held)

    own_t, oth_t = turn(own), turn(oth)
    low = jnp.full((STATS, BLOCK), LOW, jnp.float32)
    *near, stat = scores_of(0, jnp.concatenate([low, jnp.zeros_like(low)]), stacks[0:3])
    *far, stat = scores_of(3, stat, stacks[3:4])
    stat_other = moved(stat, "c", 1)

    def sums_of(wanted, stat):
        return pl.pallas_call(
            functools.partial(sum_kernel, wanted),
            in_specs=[smem] * 4 + [vmem] * 8,
            out_specs=[vmem] * (len(wanted) + 1),
            out_shape=[jax.ShapeDtypeStruct((PACK, DIM), jnp.bfloat16)] * len(wanted)
            + [jax.ShapeDtypeStruct((BLOCKS, BLOCK), jnp.float32)],
            scratch_shapes=[
                pltpu.VMEM((STATS, BLOCK), jnp.float32),
                pltpu.VMEM((32, PANEL), jnp.float32),
            ],
            compiler_params=pltpu.CompilerParams(vmem_limit_bytes=8 << 20),
            cost_estimate=pl.CostEstimate(
                flops=4_000_000_000, transcendentals=0, bytes_accessed=16_000_000
            ),
            name="sums",
        )(here, count, table, place, own, oth, stat, stat_other, *near, *far)

    pack_next, pack_last, pack_own, norm = sums_of((1, 3, 0), stat)
    pack_far, _ = sums_of((2,), stat)
    packs = [pack_own, pack_next, pack_far, pack_last]
    got = [packs[0]] + [shifted(packs[d], True, -d) for d in (1, 2, 3)]
    chunks = pl.pallas_call(
        fold_kernel,
        in_specs=[vmem] * 4,
        out_specs=[vmem] * 4,
        out_shape=[jax.ShapeDtypeStruct((CHUNK, DIM), jnp.bfloat16)] * 4,
        compiler_params=pltpu.CompilerParams(vmem_limit_bytes=8 << 20),
        name="fold",
    )(*got)
    norm, chunks = lax.optimization_barrier((norm, chunks))
    last = [homeward(chunk, d) for chunk, d in zip(chunks, ORDER)]
    part_norm = lax.dynamic_slice_in_dim(norm, c * 8, 8, axis=0)
    log_norm = swapped(part_norm).reshape(8 * BLOCK)
    revised = pl.pallas_call(
        finish_kernel,
        in_specs=[vmem] * 5,
        out_specs=vmem,
        out_shape=jax.ShapeDtypeStruct((PANEL, DIM), jnp.bfloat16),
        compiler_params=pltpu.CompilerParams(vmem_limit_bytes=4 << 20),
        name="finish",
    )(fine_cluster_means, *last)
    return (revised, log_norm)


def solution(mesh):
    split = Mesh(mesh.devices.reshape(2, 2, 2, 4, 4), ("yh", "c", "yl", "z", "x"))
    blk, row = ("yl", "z", "x"), ("yh", "c")
    return jax.shard_map(
        shards,
        mesh=split,
        in_specs=(P(blk, row), P(blk + row, None), P(blk + row, None), P()),
        out_specs=(P(blk + row, None), P(blk + row)),
        check_vma=False,
    )
```

```python
import functools
import math

import jax
import jax.numpy as jnp
from jax import lax
from jax.experimental import pallas as pl
from jax.experimental.pallas import tpu as pltpu
from jax.sharding import Mesh, PartitionSpec as P

PANEL = 128
BLOCK = 128
DIM = 1024
SLICE = 256
BLOCKS = 16
PANELS = 16
SLOTS = 8
Y = ("yh", "yl")
ORDER = (0, 1, 3, 2)
LOW = -1e30
HIGH = 1e30
LN2 = math.log(2.0)
PACK = 4 * PANEL + 8
CHUNK = PANEL + 8
STATS = 24


def moved(value, axis, by):
    size = lax.axis_size(axis)
    return lax.ppermute(value, axis, [(i, (i - by) % size) for i in range(size)])


def swapped(value):
    return lax.ppermute(value, ("c", "yl"), [(0, 0), (1, 2), (2, 1), (3, 3)])


def nt_dot(a, b):
    return lax.dot_general(a, b, (((1,), (1,)), ((), ())), preferred_element_type=jnp.float32)


def points_of(own, oth, c):
    parts = []
    for ref, core in ((own, c), (oth, 1 - c)):
        for yh in range(2):
            parts.append((ref, 16 * yh, pl.multiple_of((2 * yh + core) * SLICE, SLICE)))
    return parts


def rows_of(parts, places, features):
    return jnp.concatenate(
        [
            jnp.concatenate([ref[(place + shift) % 32] for ref, shift, _ in parts], axis=features)
            for place in places
        ],
        axis=1 - features,
    )


def by_turns(turns, run):
    for t in range(1, SLOTS // 2 + 1):
        pl.when(turns == t)(lambda t=t: run(t))


def shifted(value, first, by):
    pairs = []
    for c in range(2):
        for z in range(4):
            for x in range(4):
                along_z = (c == 0) == first
                far = ((z + by) % 4, x) if along_z else (z, (x + by) % 4)
                pairs.append((16 * c + 4 * far[0] + far[1], 16 * c + 4 * z + x))
    return lax.ppermute(value, ("c", "z", "x"), pairs)


def homeward(value, by):
    pairs = []
    for c in range(2):
        for yl in range(2):
            for z in range(4):
                for x in range(4):
                    far = (z, (x + by) % 4) if c == 0 else ((z + by) % 4, x)
                    to = 16 * (2 * yl + c) + 4 * far[0] + far[1]
                    pairs.append((16 * (2 * c + yl) + 4 * z + x, to))
    return lax.ppermute(value, ("c", "yl", "z", "x"), pairs)


def join_kernel(*refs):
    for d in range(4):
        refs[6][8 * d : 8 * d + 8] = refs[d][...]


def turn_kernel(ref, out, *kept):
    def one(i, _):
        out[i] = ref[i].T
        for copy in kept:
            copy[i] = ref[i]
        return 0

    lax.fori_loop(0, 32, one, 0, unroll=4)


def score_kernel(
    base, here_ref, count_ref, list_ref, place_ref, scale_ref, own, oth, before_ref, *refs
):
    p_in, (l_ref, top_ref, stat_ref) = refs[:-3], refs[-3:]
    twice, once = scale_ref[0], scale_ref[1]
    parts = points_of(own, oth, here_ref[1])
    stat_ref[...] = before_ref[...]

    def panel_step(i, p_ref, start):
        r = start + i
        row = r - 4 * base
        panel32 = p_ref[i].astype(jnp.float32)
        sqnorm = jnp.sum(panel32 * panel32, axis=1, keepdims=True) * once

        def run(turns):
            blocks = [list_ref[r, n] for n in range(2 * turns)]
            places = [place_ref[r, n] for n in range(2 * turns)]
            lhs = jnp.concatenate([p_ref[i, :, pl.ds(at, SLICE)] for _, _, at in parts], axis=1)
            old = jnp.concatenate([stat_ref[pl.ds(block, 1), :] for block in blocks], axis=1)
            total = jnp.concatenate(
                [stat_ref[pl.ds(STATS + block, 1), :] for block in blocks], axis=1
            )
            tops, adds = [], []
            for t in range(turns):
                lanes = slice(2 * t * BLOCK, 2 * (t + 1) * BLOCK)
                rhs = rows_of(parts, places[2 * t : 2 * t + 2], 0)
                logit = jnp.dot(lhs, rhs, preferred_element_type=jnp.float32) * twice - sqnorm
                top = jnp.maximum(old[:, lanes], jnp.max(logit, axis=0, keepdims=True))
                power = jnp.exp2(logit - top)
                l_ref[row, :, lanes] = power
                tops.append(top)
                adds.append(jnp.sum(power, axis=0, keepdims=True))
            new = jnp.concatenate(tops, axis=1)
            total = total * jnp.exp2(old - new) + jnp.concatenate(adds, axis=1)
            top_ref[row, :, 0 : 2 * turns * BLOCK] = jnp.broadcast_to(new, (8, 2 * turns * BLOCK))
            for j, block in enumerate(blocks):
                lanes = slice(j * BLOCK, (j + 1) * BLOCK)
                stat_ref[pl.ds(block, 1), :] = new[:, lanes]
                stat_ref[pl.ds(STATS + block, 1), :] = total[:, lanes]

        by_turns((count_ref[r] + 1) // 2, run)

    for k, p_ref in enumerate(p_in):

        def step(i, _, k=k, p_ref=p_ref):
            panel_step(i, p_ref, 4 * (base + k))
            return 0

        lax.fori_loop(0, 4, step, 0)


def sum_kernel(
    wanted, here_ref, count_ref, list_ref, place_ref, own, oth, mine_ref, other_ref, *refs
):
    scored, refs = ((refs[0], refs[1], 0), (refs[2], refs[3], 3)), refs[4:]
    outs, (norm_ref, full_ref, mass_ref) = dict(zip(wanted, refs)), refs[len(wanted) :]
    parts = points_of(own, oth, here_ref[1])
    m0, s0 = mine_ref[0:STATS, :], mine_ref[STATS : 2 * STATS, :]
    m1, s1 = other_ref[0:STATS, :], other_ref[STATS : 2 * STATS, :]
    top = jnp.maximum(m0, m1)
    norm = top + jnp.log(s0 * jnp.exp2(m0 - top) + s1 * jnp.exp2(m1 - top)) * (1.0 / LN2)
    norm_ref[...] = norm[0:BLOCKS, :] * LN2
    row = lax.broadcasted_iota(jnp.int32, (STATS, BLOCK), 0)
    full_ref[...] = jnp.where(row < BLOCKS, norm, HIGH)
    mass_ref[...] = jnp.zeros_like(mass_ref)

    def panel_step(k, d, l_ref, top_ref, base):
        r = 4 * k + d
        row = r - 4 * base
        rows = pl.multiple_of(k * PANEL, PANEL)
        turns = (count_ref[r] + 1) // 2

        @pl.when(turns == 0)
        def _():
            outs[d][pl.ds(rows, PANEL), :] = jnp.zeros((PANEL, DIM), jnp.bfloat16)

        def run(turns):
            blocks = [list_ref[r, n] for n in range(2 * turns)]
            places = [place_ref[r, n] for n in range(2 * turns)]
            norm = jnp.concatenate([full_ref[pl.ds(block, 1), :] for block in blocks], axis=1)
            lanes = slice(0, 2 * turns * BLOCK)
            factor = jnp.exp2(top_ref[row, 0:1, lanes] - norm)
            weight = (l_ref[row, :, lanes] * factor).astype(jnp.bfloat16)
            sums = jnp.dot(weight, rows_of(parts, places, 1), preferred_element_type=jnp.float32)
            sums = sums.astype(jnp.bfloat16)
            for i, (_, _, offset) in enumerate(parts):
                outs[d][pl.ds(rows, PANEL), pl.ds(offset, SLICE)] = sums[:, i * SLICE : (i + 1) * SLICE]
            mass = nt_dot(jnp.ones((8, 2 * turns * BLOCK), jnp.bfloat16), weight)[0:1, :]
            high = mass.astype(jnp.bfloat16).astype(jnp.float32)
            mass_ref[pl.ds(8 * d + k, 1), :] = high
            mass_ref[pl.ds(8 * d + 4 + k, 1), :] = mass - high

        by_turns(turns, run)
        return 0

    for d in wanted:
        for l_ref, top_ref, base in scored:

            def step(k, _, d=d, l_ref=l_ref, top_ref=top_ref, base=base):
                return panel_step(k, d, l_ref, top_ref, base)

            lax.fori_loop(base, 3 if base == 0 else 4, step, 0)
        outs[d][4 * PANEL :, :] = jnp.zeros((8, DIM), jnp.bfloat16)
        outs[d][4 * PANEL :, 0:PANEL] = mass_ref[8 * d : 8 * d + 8, :].astype(jnp.bfloat16)


def fold_kernel(*refs):
    ins, outs = refs[0:4], refs[4:8]
    total = sum(ref[4 * PANEL :, 0:PANEL].astype(jnp.float32) for ref in ins)
    mass = total[0:4, :] + total[4:8, :]
    high = mass.astype(jnp.bfloat16).astype(jnp.float32)
    for i in range(4):
        rows = slice(i * PANEL, (i + 1) * PANEL)
        added = sum(ref[rows, :].astype(jnp.float32) for ref in ins)
        outs[i][0:PANEL, :] = added.astype(jnp.bfloat16)
        outs[i][PANEL:, :] = jnp.zeros((8, DIM), jnp.bfloat16)
        pieces = [high[i : i + 1], mass[i : i + 1] - high[i : i + 1]]
        pieces.append(jnp.zeros((6, PANEL), jnp.float32))
        outs[i][PANEL:, 0:PANEL] = jnp.concatenate(pieces, axis=0).astype(jnp.bfloat16)


def finish_kernel(panel_ref, *refs):
    ins, out_ref = refs[0:4], refs[4]
    row = lax.broadcasted_iota(jnp.int32, (PANEL, PANEL), 0)
    lane = lax.broadcasted_iota(jnp.int32, (PANEL, PANEL), 1)
    tail = sum(ref[PANEL:, 0:PANEL].astype(jnp.float32) for ref in ins)
    mass = tail[0:1, :] + tail[1:2, :]
    column = jnp.sum(jnp.where(row == lane, mass, 0.0), axis=1, keepdims=True)
    sums = sum(ref[0:PANEL, :].astype(jnp.float32) for ref in ins)
    panel = panel_ref[...].astype(jnp.float32)
    out_ref[...] = ((sums + panel) * (1.0 / (column + 1.0))).astype(jnp.bfloat16)


def shards(coarse_cluster_means, fine_cluster_means, block_panel_candidates, softmax_heat):
    yl, c = lax.axis_index("yl"), lax.axis_index("c")
    y = 2 * lax.axis_index("yh") + yl
    z, x = lax.axis_index("z"), lax.axis_index("x")
    here = jnp.stack([y, c]).astype(jnp.int32)
    once = 1.0 / (softmax_heat * (math.sqrt(DIM) * LN2))
    scale = jnp.concatenate([2.0 * once, once])
    smem = pl.BlockSpec(memory_space=pltpu.SMEM)
    vmem = pl.BlockSpec(memory_space=pltpu.VMEM)

    panel = swapped(fine_cluster_means)
    groups = coarse_cluster_means.reshape(4, 8, BLOCK, SLICE)
    own = [lax.dynamic_index_in_dim(groups, (y - d) % 4, 0, keepdims=False) for d in range(4)]
    own[1], own[3] = moved(own[1], Y, 1), moved(own[3], Y, 3)
    stack = jnp.stack([panel] + [shifted(panel, True, d) for d in (1, 2, 3)])
    mine = swapped(block_panel_candidates)
    stack, own, mine = lax.optimization_barrier((stack, own, mine))
    own[2] = moved(own[2], Y, 2)
    other = moved(mine, "c", 1)
    stacks = [stack] + [shifted(stack, False, d) for d in ORDER[1:]]
    own = pl.pallas_call(
        join_kernel,
        in_specs=[vmem] * 4 + [pl.BlockSpec(memory_space=pl.ANY)] * 2,
        out_specs=vmem,
        out_shape=jax.ShapeDtypeStruct((32, BLOCK, SLICE), jnp.bfloat16),
        compiler_params=pltpu.CompilerParams(vmem_limit_bytes=8 << 20),
        name="join",
    )(*own, stacks[1], stacks[2])
    oth = moved(own, "c", 1)

    cands = jnp.where(c == 0, jnp.stack([mine, other]), jnp.stack([other, mine])).reshape(BLOCKS, 8)
    dz, dx = (cands // 4 % 4 - z) % 4, (cands % 4 - x) % 4
    d1, d2 = jnp.where(c == 0, dz, dx), jnp.where(c == 0, dx, dz)
    spot = 4 * jnp.where(d2 >= 2, 5 - d2, d2) + d1
    spot = jnp.where(cands // 16 == c, spot, -1)
    hits = jnp.any(spot[None] == jnp.arange(PANELS, dtype=jnp.int32)[:, None, None], axis=2)
    order = jnp.cumsum(hits.astype(jnp.int32), axis=1) - 1
    count = jnp.sum(hits.astype(jnp.int32), axis=1)
    chosen = (order[:, None, :] == jnp.arange(SLOTS, dtype=jnp.int32)[None, :, None]) & hits[:, None, :]
    table = BLOCKS + jnp.sum(
        jnp.where(chosen, jnp.arange(BLOCKS, dtype=jnp.int32)[None, None, :] - BLOCKS, 0), axis=2
    )
    place = (table // 8 - y) % 4 * 8 + table % 8

    def turn(points, kept):
        straight = [jax.ShapeDtypeStruct((32, BLOCK, SLICE), jnp.bfloat16)] * kept
        return pl.pallas_call(
            turn_kernel,
            in_specs=[vmem],
            out_specs=[vmem] * (1 + kept),
            out_shape=[jax.ShapeDtypeStruct((32, SLICE, BLOCK), jnp.bfloat16), *straight],
            compiler_params=pltpu.CompilerParams(vmem_limit_bytes=8 << 20),
            name="turn",
        )(points)

    def scores_of(base, stat, held):
        return pl.pallas_call(
            functools.partial(score_kernel, base),
            in_specs=[smem] * 5 + [vmem] * (3 + len(held)),
            out_specs=[vmem] * 3,
            out_shape=[
                jax.ShapeDtypeStruct((4 * len(held), PANEL, SLOTS * BLOCK), jnp.float32),
                jax.ShapeDtypeStruct((4 * len(held), 8, SLOTS * BLOCK), jnp.float32),
                jax.ShapeDtypeStruct((2 * STATS, BLOCK), jnp.float32),
            ],
            compiler_params=pltpu.CompilerParams(vmem_limit_bytes=8 << 20),
            name="scores",
        )(here, count, table, place, scale, own_t, oth_t, stat, *held)

    (own_t,), (oth_t, oth) = turn(own, 0), turn(oth, 1)
    low = jnp.full((STATS, BLOCK), LOW, jnp.float32)
    *near, stat = scores_of(0, jnp.concatenate([low, jnp.zeros_like(low)]), stacks[0:3])
    *far, stat = scores_of(3, stat, stacks[3:4])
    stat_other = moved(stat, "c", 1)

    def sums_of(wanted, stat):
        return pl.pallas_call(
            functools.partial(sum_kernel, wanted),
            in_specs=[smem] * 4 + [vmem] * 8,
            out_specs=[vmem] * (len(wanted) + 1),
            out_shape=[jax.ShapeDtypeStruct((PACK, DIM), jnp.bfloat16)] * len(wanted)
            + [jax.ShapeDtypeStruct((BLOCKS, BLOCK), jnp.float32)],
            scratch_shapes=[
                pltpu.VMEM((STATS, BLOCK), jnp.float32),
                pltpu.VMEM((32, PANEL), jnp.float32),
            ],
            compiler_params=pltpu.CompilerParams(vmem_limit_bytes=8 << 20),
            cost_estimate=pl.CostEstimate(
                flops=4_000_000_000, transcendentals=0, bytes_accessed=16_000_000
            ),
            name="sums",
        )(here, count, table, place, own, oth, stat, stat_other, *near, *far)

    pack_far, norm = sums_of((2,), stat)
    after = lax.optimization_barrier((stat, pack_far))[0]
    pack_next, pack_last, pack_own, _ = sums_of((1, 3, 0), after)
    packs = [pack_own, pack_next, pack_far, pack_last]
    got = [packs[0]] + [shifted(packs[d], True, -d) for d in (1, 2, 3)]
    chunks = pl.pallas_call(
        fold_kernel,
        in_specs=[vmem] * 4,
        out_specs=[vmem] * 4,
        out_shape=[jax.ShapeDtypeStruct((CHUNK, DIM), jnp.bfloat16)] * 4,
        compiler_params=pltpu.CompilerParams(vmem_limit_bytes=8 << 20),
        name="fold",
    )(*got)
    norm, chunks = lax.optimization_barrier((norm, chunks))
    last = [homeward(chunk, d) for chunk, d in zip(chunks, ORDER)]
    part_norm = lax.dynamic_slice_in_dim(norm, c * 8, 8, axis=0)
    log_norm = swapped(part_norm).reshape(8 * BLOCK)
    revised = pl.pallas_call(
        finish_kernel,
        in_specs=[vmem] * 5,
        out_specs=vmem,
        out_shape=jax.ShapeDtypeStruct((PANEL, DIM), jnp.bfloat16),
        compiler_params=pltpu.CompilerParams(vmem_limit_bytes=4 << 20),
        name="finish",
    )(fine_cluster_means, *last)
    return (revised, log_norm)


def solution(mesh):
    split = Mesh(mesh.devices.reshape(2, 2, 2, 4, 4), ("yh", "c", "yl", "z", "x"))
    blk, row = ("yl", "z", "x"), ("yh", "c")
    return jax.shard_map(
        shards,
        mesh=split,
        in_specs=(P(blk, row), P(blk + row, None), P(blk + row, None), P()),
        out_specs=(P(blk + row, None), P(blk + row)),
        check_vma=False,
    )
```
